256 devices in a mesh: section: 2 (over core), srv: 32 (over x, z), tp: 4 (over y).
Axes of the slice: x: 4, y: 4, z: 8, core: 2. Of those that a mesh axis runs over, the one named last changes fastest.
Arguments:
- queries: bfloat16 [8192, 4096], P(('section', 'srv'), 'tp'), may hold values from -40 to 40
- keys: bfloat16 [8192, 512], P(('section', 'srv'), 'tp'), may hold values from -40 to 40
- values: bfloat16 [8192, 512], P(('section', 'srv'), 'tp'), may hold values from -6 to 6
- residual: bfloat16 [8192, 4096], P(('section', 'srv'), 'tp'), may hold values from -6 to 6
- out_weight: bfloat16 [4096, 4096], P('tp', ('section', 'srv')), may hold values from -0.1875 to 0.1875
- norm_gain: float32 [4096], P('tp'), may hold values from 0.25 to 1.75
- level_shift: float32 [8, 4096], P(None, 'tp'), may hold values from -3 to 3
- doc_lengths: int32 [2, 4], P('section'), may hold values from 1 to 128, 256 in all within a row
- noise_level: int32 [2, 4], P('section'), may hold values from 0 to 7
Outputs:
- normed: bfloat16 [8192, 4096], P(('section', 'srv'), 'tp')
The draws below stay inside these ranges and needn't reach their ends.
Inputs may be any that keep to these rules, and one draw needn't show every extreme that they name: `doc_lengths`: each micro-batch's lengths sum to 256.
All inputs are finite; a program needn't handle non-finite values.
Results may differ from the reference program's by a relative error of at most 0.013.
Values may be sent and summed in bfloat16 or wider, within the bound.
A program may use at most 64 MiB of HBM per device.

```python
import math
import jax
import jax.numpy as jnp
import numpy as np
from jax import lax

D = 4096
QUERY_HEADS = 32
KEY_VALUE_HEADS = 4
HEAD_SIZE = 128
BLK = 16
DOCS = 4
LEVELS = 8
MICRO_BATCH_ROWS = 4096
TOTAL_ROWS = 8192
NBLK = 256
N_SECTION = 2


def random_base_keys(key):
    drawn_samples = jax.random.normal(jax.random.fold_in(key, 11), (TOTAL_ROWS, KEY_VALUE_HEADS * HEAD_SIZE), jnp.float32)
    return drawn_samples


def draw_keys(key, part):
    return random_base_keys(key).astype(jnp.bfloat16)


def draw_queries(key, part):
    drawn_samples = jax.random.normal(jax.random.fold_in(key, 12), (TOTAL_ROWS, QUERY_HEADS * HEAD_SIZE), jnp.float32)
    return drawn_samples.astype(jnp.bfloat16)


def plant(drawn, rng, low, high):
    longest = drawn.shape.index(max(drawn.shape))
    spots = []
    for shift in (0, 1):
        where = [jax.random.randint(jax.random.fold_in(rng, axis), (), 0, length) for axis, length in enumerate(drawn.shape)]
        where[longest] = (where[longest] + shift) % drawn.shape[longest]
        spots.append(tuple(where))
    return drawn.at[spots[0]].set(low).at[spots[1]].set(high)


def steps_of(rng, extent, cuts, smallest, high):
    factor_of, own = 1.0, jax.random.fold_in(rng, 6)
    for dim, blocks in cuts:
        draws = jnp.exp(jax.random.uniform(jax.random.fold_in(own, dim), (blocks,), jnp.float32, smallest / len(cuts), high / len(cuts)))
        factor_of = factor_of * jnp.repeat(draws, extent[dim] // blocks).reshape([-1 if axis == dim else 1 for axis in range(len(extent))])
    return factor_of


def split_up(count, total, reach, lean):
    weights = [(1 << 20) // math.isqrt(rank ** lean) + 1 for rank in range(2, count + 1)]
    spare, holding = total - reach - (count - 1), [1] * (count - 1)
    while spare > 0:
        free = [i for i in range(count - 1) if holding[i] < reach]
        whole, left = sum([weights[i] for i in free]), spare
        for i in free:
            addition = min(reach - holding[i], max(1, left * weights[i] // whole), spare)
            holding[i] = holding[i] + addition
            spare = spare - addition
    return np.array([reach] + holding)


def uneven(key, count, total, reach, skew):
    if count == 2:
        one = jax.random.randint(key, (), max(1, total - reach), min(reach, total - 1) + 1)
        return jnp.stack([one, total - one])
    tallies = jnp.asarray(split_up(count, total, reach, skew), jnp.int32)
    pairs = (count - 1) // 2
    source_of, taker = tallies[1:1 + 2 * pairs:2], tallies[2:2 + 2 * pairs:2]
    margin = jnp.minimum(source_of - 1, reach - taker)
    passed = jax.random.randint(jax.random.fold_in(key, 1), (pairs,), 0, 1 << 20) % (margin + 1)
    tallies = tallies.at[1:1 + 2 * pairs:2].set(source_of - passed).at[2:2 + 2 * pairs:2].set(taker + passed)
    return tallies[jax.random.permutation(jax.random.fold_in(key, 2), count)]


def centred(rng, extent, scale, most, cuts=(), kind=jnp.bfloat16):
    values = scale * jax.random.normal(rng, extent, jnp.float32)
    if cuts:
        values = values * steps_of(rng, extent, cuts, -0.22, 0.18)
    return jnp.clip(values, -most, most).astype(kind)


def setup_inputs(seed: int = 0) -> dict:
    splits = jax.random.split(jax.random.key(seed), 10)
    return {
        "queries": draw_queries(jax.random.fold_in(splits[9], 71), 0),
        "keys": draw_keys(jax.random.fold_in(splits[9], 71), 0),
        "values": centred(splits[2], (TOTAL_ROWS, KEY_VALUE_HEADS * HEAD_SIZE), 1.0, 6.0, ((0, 64), (1, 4))),
        "residual": centred(splits[3], (TOTAL_ROWS, D), 1.0, 6.0, ((0, 64), (1, 4))),
        "out_weight": centred(splits[4], (QUERY_HEADS * HEAD_SIZE, D), (QUERY_HEADS * HEAD_SIZE // 4) ** -0.5, 0.1875, ((0, 4), (1, 64))),
        "norm_gain": jnp.clip(1.0 + 0.15 * jax.random.normal(splits[5], (D,), jnp.float32), 0.25, 1.75),
        "level_shift": centred(splits[6], (LEVELS, D), 0.5, 3.0, ((1, 4),), jnp.float32),
        "doc_lengths": jax.vmap(lambda own: uneven(own, DOCS, NBLK, NBLK // 2, 2))(jax.random.split(splits[7], N_SECTION)).reshape((N_SECTION, DOCS)).astype(jnp.int32),
        "noise_level": plant(jax.random.randint(splits[8], (N_SECTION, DOCS), 0, LEVELS), jax.random.fold_in(splits[8], 1), 0, LEVELS - 1).astype(jnp.int32),
    }


def layout(lengths_blocks):
    lengths = lengths_blocks * BLK
    ends = jnp.cumsum(lengths).astype(jnp.int32)
    starts = (ends - lengths).astype(jnp.int32)
    positions = jnp.arange(MICRO_BATCH_ROWS, dtype=jnp.int32)
    member = (positions[:, None] >= starts[None, :]) & (positions[:, None] < ends[None, :])
    first = lax.optimization_barrier(jnp.sum(jnp.where(member, starts[None, :], 0), axis=1)).astype(jnp.int32)
    limit = (positions // BLK + 1) * BLK
    return (member, first, limit.astype(jnp.int32))

def attend(queries, keys, values, first, limit):
    query_groups = QUERY_HEADS // KEY_VALUE_HEADS
    current_block = 512
    scale = HEAD_SIZE ** (-0.5)
    gathered_keys = keys.astype(jnp.float32).reshape(MICRO_BATCH_ROWS, KEY_VALUE_HEADS, HEAD_SIZE)
    gathered_values = values.astype(jnp.float32).reshape(MICRO_BATCH_ROWS, KEY_VALUE_HEADS, HEAD_SIZE)
    columns = jnp.arange(MICRO_BATCH_ROWS, dtype=jnp.int32)

    def one_block(index):
        begin = (index * current_block).astype(jnp.int32)
        query_rows = lax.dynamic_slice_in_dim(queries, begin, current_block, 0).astype(jnp.float32)
        query_rows = query_rows.reshape(current_block, KEY_VALUE_HEADS, query_groups, HEAD_SIZE)
        lower = lax.dynamic_slice_in_dim(first, begin, current_block, 0)
        upper = lax.dynamic_slice_in_dim(limit, begin, current_block, 0)
        mask = (columns[None, :] >= lower[:, None]) & (columns[None, :] < upper[:, None])
        outputs = []
        for head_number in range(KEY_VALUE_HEADS):
            scores = jnp.einsum('rgd,jd->grj', query_rows[:, head_number], gathered_keys[:, head_number]) * scale
            scores = jnp.where(mask[None], scores, -1e+30)
            best = lax.optimization_barrier(jnp.max(scores, axis=-1, keepdims=True))
            weights = jnp.where(mask[None], jnp.exp(scores - best), 0.0)
            total = lax.optimization_barrier(jnp.sum(weights, axis=-1))
            rounded = weights.astype(jnp.bfloat16).astype(jnp.float32)
            summed = jnp.einsum('grj,jd->grd', rounded, gathered_values[:, head_number])
            outputs.append(summed / total[..., None])
        stacked = jnp.stack(outputs, axis=0)
        return stacked.transpose(2, 0, 1, 3).reshape(current_block, QUERY_HEADS * HEAD_SIZE).astype(jnp.bfloat16)
    pieces = lax.map(one_block, jnp.arange(MICRO_BATCH_ROWS // current_block, dtype=jnp.int32))
    return pieces.reshape(MICRO_BATCH_ROWS, QUERY_HEADS * HEAD_SIZE)

def reference(queries, keys, values, residual, out_weight, norm_gain, level_shift, doc_lengths, noise_level):
    results = []
    for section_index in range(N_SECTION):
        lo = section_index * MICRO_BATCH_ROWS
        hi = lo + MICRO_BATCH_ROWS
        member, first, limit = layout(doc_lengths[section_index])
        attended = attend(queries[lo:hi], keys[lo:hi], values[lo:hi], first, limit)
        hidden = residual[lo:hi].astype(jnp.float32) + jnp.dot(attended, out_weight, preferred_element_type=jnp.float32)
        squares = lax.optimization_barrier(jnp.mean(hidden * hidden, axis=1))
        level = lax.optimization_barrier(jnp.sum(jnp.where(member, noise_level[section_index][None, :], 0), axis=1)).astype(jnp.int32)
        onehot = (level[:, None] == jnp.arange(LEVELS, dtype=jnp.int32)[None, :]).astype(jnp.float32)
        shift = jnp.dot(onehot, level_shift, precision=lax.Precision.HIGHEST)
        normed = hidden * lax.rsqrt(squares + 1e-06)[:, None] * norm_gain[None, :] * (1.0 + shift)
        results.append(normed.astype(jnp.bfloat16))
    return jnp.concatenate(results, axis=0)
```

```python
import functools

import jax
import jax.numpy as jnp
from jax import lax
from jax.experimental import pallas as pl
from jax.experimental.pallas import tpu as pltpu
from jax.sharding import PartitionSpec as P

D = 4096
HEAD = 128
BLK = 16
ROWS = 128
NX = 4
NZ = 8
NT = 4
PR = 32
MESH = pl.DeviceIdType.MESH
NEG = -1e30
LOG2E = 1.4426950408889634


def arrive(sem, ref):
    pltpu.make_async_copy(ref, ref, sem).wait()


def nt_dot(a, b):
    return lax.dot_general(a, b, (((1,), (1,)), ((), ())), preferred_element_type=jnp.float32)


def kernel(
    doc_ref, noise_ref, q_ref, k_ref, v_ref, res_ref, wt_ref, gain_ref, shift_ref, out_ref,
    kv, w, bias, m_s, l_s, acc, ab, ob, rb, hid, sq,
    skz, skx1, skx2, sp1, spf, spb, sqf, sqb, sqx, sa, so, ss,
    rkz, rk1, rk2, rp1, rp, rq, rqx, ra, ro, rs,
):
    sec = lax.axis_index("section")
    i = lax.axis_index("srv")
    t = lax.axis_index("tp")
    x = i // NZ
    z = i % NZ
    sgn = 1 - 2 * sec

    def dev(dx=0, dz=0):
        return (sec, ((x + dx + NX) % NX) * NZ + (z + dz + 2 * NZ) % NZ, t)

    def zmod(a):
        return (a + 2 * NZ) % NZ

    def send(src, dst, s, r, to):
        pltpu.make_async_remote_copy(
            src_ref=src, dst_ref=dst, send_sem=s, recv_sem=r, device_id=to, device_id_type=MESH
        ).start()

    kv[x, z, 0] = k_ref[...]
    kv[x, z, 1] = v_ref[...]
    w[x, z] = wt_ref[...]

    peers = [dev(dx=1), dev(dx=-1), dev(dx=2), dev(dz=1), dev(dz=-1), dev(dz=2), dev(dz=-2)]
    peers += [(sec, i, (t + d) % NT) for d in (1, 2, 3)]
    peers += [(1 - sec, i, (t + d) % NT) for d in (0, 1, 2, 3)]
    barrier = pltpu.get_barrier_semaphore()
    for peer in peers:
        pl.semaphore_signal(barrier, inc=1, device_id=peer, device_id_type=MESH)
    pl.semaphore_wait(barrier, len(peers))

    def kv_along_x(zz):
        @pl.when(x < NX - 1)
        def _():
            send(kv.at[x, zz], kv.at[x, zz], skx1.at[zz], rk1.at[zz], dev(dx=1))

        @pl.when((x < NX - 2) & (zz >= z))
        def _():
            send(kv.at[x, zz], kv.at[x, zz], skx2.at[zz], rk2.at[zz], dev(dx=2))

    def late_along_x(zz):
        piece = w.at[x, zz, pl.ds(PR, 64 - PR)]
        for n, dx in enumerate((1, -1, 2)):
            send(piece, piece, sqx.at[n], rqx.at[n], dev(dx=dx))

    for n, dz in enumerate((1, -1, 2, -2)):
        send(kv.at[x, z], kv.at[x, z], skz.at[n], rkz.at[z], dev(dz=dz))
    kv_along_x(z)
    early = w.at[x, z, pl.ds(0, PR)]
    for n, dx in enumerate((1, -1, 2)):
        send(early, early, sp1.at[n], rp1.at[n], dev(dx=dx))
    late = w.at[x, z, pl.ds(PR, 64 - PR)]
    send(late, late, sqf.at[0], rq.at[z], dev(dz=sgn))
    send(late, late, sqb.at[0], rq.at[z], dev(dz=-sgn))
    late_along_x(z)

    def kv_here(dz):
        zz = zmod(z + dz)
        arrive(rkz.at[zz], kv.at[x, zz])
        return zz

    def early_out(zz, xx, sem_f, sem_b, forward, backward):
        piece = w.at[xx, zz, pl.ds(0, PR)]
        if forward:
            send(piece, piece, sem_f, rp.at[zz, xx], dev(dz=sgn))
        if backward:
            send(piece, piece, sem_b, rp.at[zz, xx], dev(dz=-sgn))

    def late_step(k):
        zf = zmod(z - sgn * k)
        piece = w.at[x, zf, pl.ds(PR, 64 - PR)]
        arrive(rq.at[zf], piece)
        if k <= 3:
            send(piece, piece, sqf.at[k], rq.at[zf], dev(dz=sgn))
        late_along_x(zf)
        if k <= 3:
            zb = zmod(z + sgn * k)
            piece = w.at[x, zb, pl.ds(PR, 64 - PR)]
            arrive(rq.at[zb], piece)
            if k <= 2:
                send(piece, piece, sqb.at[k], rq.at[zb], dev(dz=-sgn))
            late_along_x(zb)

    kv_along_x(kv_here(-1))
    kv_along_x(kv_here(1))
    left = kv_here(-2)
    send(kv.at[x, left], kv.at[x, left], skz.at[4], rkz.at[left], dev(dz=1))
    right = kv_here(2)
    send(kv.at[x, right], kv.at[x, right], skz.at[5], rkz.at[right], dev(dz=-1))
    far = zmod(z - 2 * sgn)
    send(kv.at[x, far], kv.at[x, far], skz.at[6], rkz.at[far], dev(dz=2 * sgn))
    kv_along_x(left)
    kv_along_x(right)

    for n, dx in enumerate((1, -1, 2)):
        arrive(rp1.at[n], w.at[(x - dx + NX) % NX, z, pl.ds(0, PR)])

    def first_out(xx, c):
        early_out(z, xx, spf.at[0, xx], spb.at[0, xx], True, True)
        return c

    lax.fori_loop(0, NX, first_out, 0)
    late_step(1)
    kv_along_x(kv_here(-3))
    kv_along_x(kv_here(3))
    kv_along_x(kv_here(4))

    row = i * ROWS + lax.broadcasted_iota(jnp.int32, (ROWS, 1), 0)
    starts, ends, at = [], [], jnp.int32(0)
    for d in range(4):
        starts.append(at)
        at = at + doc_ref[0, d] * BLK
        ends.append(at)
    member = [(row >= starts[d]) & (row < ends[d]) for d in range(4)]
    first = jnp.zeros((ROWS, 1), jnp.int32)
    for d in range(4):
        first = jnp.where(member[d], starts[d], first)
    limit = (row // BLK + 1) * BLK

    def mask_of(xx):
        key = xx * (NZ * ROWS) + lax.broadcasted_iota(jnp.int32, (ROWS, NZ * ROWS), 1)
        bias[...] = jnp.where((key >= first) & (key < limit), 0.0, NEG)

    def unit(xx, h, opening):
        q = q_ref[:, pl.ds(pl.multiple_of(h * HEAD, HEAD), HEAD)]
        keys = kv[xx, :, 0].reshape(NZ * ROWS, HEAD)
        vals = kv[xx, :, 1].reshape(NZ * ROWS, HEAD)
        s = nt_dot(q, keys) * (HEAD ** -0.5 * LOG2E) + bias[...]
        best = jnp.max(s, axis=1, keepdims=True)
        if not opening:
            old = m_s[h][:, :1]
            best = jnp.maximum(best, old)
        p = jnp.exp2(s - best)
        total = jnp.sum(p, axis=1, keepdims=True)
        summed = jnp.dot(p.astype(jnp.bfloat16), vals, preferred_element_type=jnp.float32)
        if not opening:
            alpha = jnp.exp2(old - best)
            total = total + alpha * l_s[h][:, :1]
            summed = summed + alpha * acc[h]
        m_s[h] = jnp.broadcast_to(best, (ROWS, HEAD))
        l_s[h] = jnp.broadcast_to(total, (ROWS, HEAD))
        acc[h] = summed

    def early_step(k, compute):
        def one(xx, c):
            zf = zmod(z - sgn * k)
            arrive(rp.at[zf, xx], w.at[xx, zf, pl.ds(0, PR)])
            if k <= 3:
                early_out(zf, xx, spf.at[min(k, 3), xx], None, True, False)
            if k <= 3:
                zb = zmod(z + sgn * k)
                arrive(rp.at[zb, xx], w.at[xx, zb, pl.ds(0, PR)])
                if k <= 2:
                    early_out(zb, xx, None, spb.at[min(k, 2), xx], False, True)
            if compute is not None:
                compute(2 * xx)
                compute(2 * xx + 1)
            return c

        lax.fori_loop(0, NX, one, 0)

    mask_of(x)
    early_step(1, lambda h: unit(x, h, True))
    late_step(2)

    @pl.when(x >= 1)
    def _():
        def one(zz, c):
            arrive(rk1.at[zz], kv.at[x - 1, zz])
            return c

        lax.fori_loop(0, NZ, one, 0)
        mask_of(x - 1)

    def second(h):
        @pl.when(x >= 1)
        def _():
            unit(x - 1, h, False)

    early_step(2, second)
    late_step(3)

    @pl.when(x >= 2)
    def _():
        def one(zz, c):
            @pl.when(zz >= z)
            def _():
                arrive(rk2.at[zz], kv.at[x - 2, zz])

            @pl.when(zz < z)
            def _():
                kv[x - 2, zz] = jnp.zeros((2, ROWS, HEAD), jnp.bfloat16)

            return c

        lax.fori_loop(0, NZ, one, 0)
        mask_of(x - 2)

    def third(h):
        @pl.when(x >= 2)
        def _():
            unit(x - 2, h, False)

    early_step(3, third)
    late_step(4)

    def attended(h, c):
        ab[sec, :, pl.ds(pl.multiple_of(h * HEAD, HEAD), HEAD)] = (acc[h] / l_s[h]).astype(jnp.bfloat16)
        return c

    lax.fori_loop(0, 8, attended, 0)
    send(ab.at[sec], ab.at[sec], sa.at[0], ra.at[0], (1 - sec, i, t))
    early_step(4, None)
    for n, dx in enumerate((1, -1, 2)):
        arrive(rqx.at[n], w.at[(x - dx + NX) % NX, :, pl.ds(PR, 64 - PR)])
    arrive(ra.at[0], ab.at[1 - sec])

    half = z // 2

    def pair_of(n):
        return (half + n) % 4

    def project(n, c):
        pp = pair_of(n)

        def one(xx, c):
            block = w[xx, pl.ds(2 * pp, 2)].reshape(ROWS, NT * 256)
            o = nt_dot(ab[...].reshape(2 * ROWS, NT * 256), block)
            ob[xx // 2, pp, 0, xx % 2] = o[:ROWS].astype(jnp.bfloat16)
            ob[xx // 2, pp, 1, xx % 2] = o[ROWS:].astype(jnp.bfloat16)
            return c

        lax.fori_loop(0, NX, one, 0)
        for tl in range(2):
            for s2 in range(2):
                to = 2 * sec + tl
                mine = (sec == s2) & (to == t)

                @pl.when(mine)
                def _():
                    pltpu.make_async_copy(ob.at[tl, pp, s2], rb.at[t, pp], ro.at[t, pp]).start()

                @pl.when(jnp.logical_not(mine))
                def _():
                    send(
                        ob.at[tl, pp, s2], rb.at[t, pp], so.at[tl, pp, s2], ro.at[t, pp], (jnp.int32(s2), i, to)
                    )

        return c

    lax.fori_loop(0, 4, project, 0)

    def gathered(n, squares):
        pp = pair_of(n)
        for ts in range(NT):
            arrive(ro.at[ts, pp], rb.at[ts, pp])
        for lo in range(2):
            cols = pl.ds(pl.multiple_of(lo * 512 + pp * 128, 128), 128)
            h = res_ref[:, cols].astype(jnp.float32)
            for ts in range(NT):
                h = h + rb[ts, pp, lo].astype(jnp.float32)
            hid[:, cols] = h
            squares = squares + h * h
        return squares

    squares = lax.fori_loop(0, 4, gathered, jnp.zeros((ROWS, 128), jnp.float32))
    column = jnp.broadcast_to(jnp.sum(squares, axis=1, keepdims=True), (ROWS, 128))
    sq[t] = jnp.transpose(column)[:8]
    for n, d in enumerate((1, 2, 3)):
        send(sq.at[t], sq.at[t], ss.at[n], rs.at[n], (sec, i, (t + d) % NT))
    gains = []
    for d in range(4):
        gains.append(gain_ref[...] * (1.0 + shift_ref[pl.ds(noise_ref[0, d], 1), :]))
    for n, d in enumerate((1, 2, 3)):
        arrive(rs.at[n], sq.at[(t - d + NT) % NT])
    whole = sq[0] + sq[1] + sq[2] + sq[3]
    inverse = jnp.transpose(jnp.broadcast_to(lax.rsqrt(whole[:1] / D + 1e-6), (ROWS, 128)))
    for c in range(8):
        cols = slice(c * 128, c * 128 + 128)
        g = jnp.broadcast_to(gains[0][:, cols], (ROWS, 128))
        for d in range(1, 4):
            g = jnp.where(member[d], gains[d][:, cols], g)
        out_ref[:, cols] = (hid[:, cols] * inverse * g).astype(jnp.bfloat16)

    for n in range(7):
        arrive(skz.at[n], kv.at[0, 0])

    def drain(zz, c):
        @pl.when(x < NX - 1)
        def _():
            arrive(skx1.at[zz], kv.at[0, 0])

        @pl.when((x < NX - 2) & (zz >= z))
        def _():
            arrive(skx2.at[zz], kv.at[0, 0])

        return c

    lax.fori_loop(0, NZ, drain, 0)
    for n in range(3):
        arrive(sp1.at[n], w.at[0, 0, pl.ds(0, PR)])
        arrive(sqx.at[n], w.at[0, :, pl.ds(PR, 64 - PR)])
        arrive(ss.at[n], sq.at[0])

    def drain_early(xx, c):
        for k in range(4):
            arrive(spf.at[k, xx], w.at[0, 0, pl.ds(0, PR)])
        for k in range(3):
            arrive(spb.at[k, xx], w.at[0, 0, pl.ds(0, PR)])
        return c

    lax.fori_loop(0, NX, drain_early, 0)
    for k in range(4):
        arrive(sqf.at[k], w.at[0, 0, pl.ds(PR, 64 - PR)])
    for k in range(3):
        arrive(sqb.at[k], w.at[0, 0, pl.ds(PR, 64 - PR)])
    arrive(sa.at[0], ab.at[0])

    def drain_out(pp, c):
        for tl in range(2):
            for s2 in range(2):
                mine = (sec == s2) & (2 * sec + tl == t)

                @pl.when(jnp.logical_not(mine))
                def _():
                    arrive(so.at[tl, pp, s2], rb.at[0, 0])

        return c

    lax.fori_loop(0, 4, drain_out, 0)


def on_device(queries, keys, values, residual, out_weight, norm_gain, level_shift, doc_lengths, noise_level):
    bf, f32, sem = jnp.bfloat16, jnp.float32, pltpu.SemaphoreType.DMA
    vm = pl.BlockSpec(memory_space=pltpu.VMEM)
    sm = pl.BlockSpec(memory_space=pltpu.SMEM)
    return pl.pallas_call(
        kernel,
        out_shape=jax.ShapeDtypeStruct((ROWS, 1024), bf),
        in_specs=[sm, sm] + [vm] * 7,
        out_specs=vm,
        scratch_shapes=[
            pltpu.VMEM((NX, NZ, 2, ROWS, HEAD), bf),
            pltpu.VMEM((NX, NZ, 64, 1024), bf),
            pltpu.VMEM((ROWS, NZ * ROWS), f32),
            pltpu.VMEM((8, ROWS, HEAD), f32),
            pltpu.VMEM((8, ROWS, HEAD), f32),
            pltpu.VMEM((8, ROWS, HEAD), f32),
            pltpu.VMEM((2, ROWS, 1024), bf),
            pltpu.VMEM((2, 4, 2, 2, ROWS, 128), bf),
            pltpu.VMEM((NT, 4, 2, ROWS, 128), bf),
            pltpu.VMEM((ROWS, 1024), f32),
            pltpu.VMEM((NT, 8, 128), f32),
            sem((7,)), sem((NZ,)), sem((NZ,)), sem((3,)), sem((4, NX)), sem((3, NX)),
            sem((4,)), sem((3,)), sem((3,)), sem((1,)), sem((2, 4, 2)), sem((3,)),
            sem((NZ,)), sem((NZ,)), sem((NZ,)), sem((3,)), sem((NZ, NX)), sem((NZ,)),
            sem((3,)), sem((1,)), sem((NT, 4)), sem((3,)),
        ],
        compiler_params=pltpu.CompilerParams(
            collective_id=0, has_side_effects=True, vmem_limit_bytes=40 << 20
        ),
    )(
        doc_lengths, noise_level, queries, keys, values, residual, out_weight.T,
        norm_gain.reshape(1, 1024), level_shift,
    )


def solution(mesh):
    placed = (
        P(("section", "srv"), "tp"),
        P(("section", "srv"), "tp"),
        P(("section", "srv"), "tp"),
        P(("section", "srv"), "tp"),
        P("tp", ("section", "srv")),
        P("tp"),
        P(None, "tp"),
        P("section", None),
        P("section", None),
    )
    return jax.shard_map(
        on_device,
        mesh=mesh,
        in_specs=placed,
        out_specs=P(("section", "srv"), "tp"),
        check_vma=False,
    )
```

```python
import functools

import jax
import jax.numpy as jnp
from jax import lax
from jax.experimental import pallas as pl
from jax.experimental.pallas import tpu as pltpu
from jax.sharding import PartitionSpec as P

D = 4096
HEAD = 128
BLK = 16
ROWS = 128
NX = 4
NZ = 8
NT = 4
MESH = pl.DeviceIdType.MESH
NEG = -1e30
LOG2E = 1.4426950408889634


def arrive(sem, ref):
    pltpu.make_async_copy(ref, ref, sem).wait()


def nt_dot(a, b):
    return lax.dot_general(a, b, (((1,), (1,)), ((), ())), preferred_element_type=jnp.float32)


def kernel(
    doc_in, noise_in, q_in, k_in, v_in, res_in, wt_in, gain_in, shift_in, out_ref,
    doc_ref, noise_ref, q_ref, res_ref, gain_ref, shift_ref,
    kv, w, bias, m_s, l_s, acc, ab, ob, rb, hid, sq,
    sin, skz, skx1, sxx, sk2, swx, swf, swb, swd, sa, so, ss,
    rkz, rk1, rk2, rwx, rw, rwd, ra, ro, rs,
):
    sec = lax.axis_index("section")
    i = lax.axis_index("srv")
    t = lax.axis_index("tp")
    x = i // NZ
    z = i % NZ
    sgn = 1 - 2 * sec

    def dev(dx=0, dz=0):
        return (sec, ((x + dx + NX) % NX) * NZ + (z + dz + 2 * NZ) % NZ, t)

    def zmod(a):
        return (a + 2 * NZ) % NZ

    def send(src, dst, s, r, to):
        pltpu.make_async_remote_copy(
            src_ref=src, dst_ref=dst, send_sem=s, recv_sem=r, device_id=to, device_id_type=MESH
        ).start()

    peers = [dev(dz=1), dev(dz=-1), dev(dz=2), dev(dz=-2), (1 - sec, i, t)]
    peers.append(dev(dx=2))
    for dx in (-1, 0, 1):
        for d in range(NT):
            if dx or d:
                peers.append((sec, ((x + dx + NX) % NX) * NZ + z, (t + d) % NT))
    barrier = pltpu.get_barrier_semaphore()
    for peer in peers:
        pl.semaphore_signal(barrier, inc=1, device_id=peer, device_id_type=MESH)
    loads = [
        pltpu.make_async_copy(src, dst, sin.at[n])
        for n, (src, dst) in enumerate((
            (k_in, kv.at[x, z, 0]),
            (v_in, kv.at[x, z, 1]),
            (wt_in, w.at[0, sec, z]),
            (doc_in, doc_ref),
            (noise_in, noise_ref),
            (q_in, q_ref),
            (gain_in, gain_ref),
            (shift_in, shift_ref),
            (res_in, res_ref),
        ))
    ]
    for load in loads:
        load.start()
    for load in loads[:3]:
        load.wait()
    pl.semaphore_wait(barrier, len(peers))

    def kv_along_x(zz):
        @pl.when(x < NX - 1)
        def _():
            send(kv.at[x, zz], kv.at[x, zz], skx1.at[zz], rk1.at[zz], dev(dx=1))

    def when_send(cond, zz, n, dz):
        @pl.when(cond)
        def _():
            send(kv.at[x - 2, zz], kv.at[x - 2, zz], sk2.at[n], rk2.at[zz], dev(dz=dz))

    def when_here(cond, zz):
        @pl.when(cond)
        def _():
            arrive(rk2.at[zz], kv.at[x - 2, zz])

    def need(zz, d):
        return (x >= 2) & (zmod(zz + d) < zz)

    def by_two(zz, side):
        return need(zz, 2 * side) | need(zz, 3 * side) | (need(zz, 4) & (sgn == side))

    def old_first():
        when_here(x >= 2, z)
        when_send(need(z, 1), z, 0, 1)
        when_send(need(z, -1), z, 1, -1)
        when_send(by_two(z, 1), z, 2, 2)
        when_send(by_two(z, -1), z, 3, -2)

    def old_second():
        for side in (1, -1):
            zz = zmod(z - 2 * side)
            when_here(by_two(zz, side), zz)
            when_send(need(zz, 3 * side), zz, 4 + (1 - side) // 2, side)
        zz = zmod(z - 2 * sgn)
        when_send(need(zz, 4), zz, 6, 2 * sgn)

    def old_last():
        for d in (1, -1, 3, -3, 4):
            zz = zmod(z - d)
            when_here(need(zz, d), zz)

    for n, dz in enumerate((1, -1, 2, -2)):
        send(kv.at[x, z], kv.at[x, z], skz.at[n], rkz.at[z], dev(dz=dz))
    kv_along_x(z)

    @pl.when(x < NX - 2)
    def _():
        send(kv.at[x, z], kv.at[x, z], sxx.at[0], rk2.at[z], dev(dx=2))

    def kv_here(dz):
        zz = zmod(z + dz)
        arrive(rkz.at[zz], kv.at[x, zz])
        return zz

    def across():
        send(w.at[0, sec, z], w.at[1, sec, z], swx.at[0], rwx.at[0], dev(dx=2))

    def own_out(cl):
        piece = w.at[cl, sec, z]
        if cl:
            arrive(rwx.at[0], piece)
        send(piece, piece, swf.at[cl, 0], rw.at[cl, z], dev(dz=sgn))
        send(piece, piece, swb.at[cl, 0], rw.at[cl, z], dev(dz=-sgn))
        send(piece, piece, swd.at[cl, z], rwd.at[cl, z], (1 - sec, i, t))

    def ring(cl, k):
        zf = zmod(z - sgn * k)
        piece = w.at[cl, sec, zf]
        arrive(rw.at[cl, zf], piece)
        if k <= 3:
            send(piece, piece, swf.at[cl, k], rw.at[cl, zf], dev(dz=sgn))
        send(piece, piece, swd.at[cl, zf], rwd.at[cl, zf], (1 - sec, i, t))
        if k <= 3:
            zb = zmod(z + sgn * k)
            piece = w.at[cl, sec, zb]
            arrive(rw.at[cl, zb], piece)
            if k <= 2:
                send(piece, piece, swb.at[cl, k], rw.at[cl, zb], dev(dz=-sgn))
            send(piece, piece, swd.at[cl, zb], rwd.at[cl, zb], (1 - sec, i, t))

    def near():
        kv_along_x(kv_here(-1))
        kv_along_x(kv_here(1))
        left = kv_here(-2)
        send(kv.at[x, left], kv.at[x, left], skz.at[4], rkz.at[left], dev(dz=1))
        right = kv_here(2)
        send(kv.at[x, right], kv.at[x, right], skz.at[5], rkz.at[right], dev(dz=-1))
        far = zmod(z - 2 * sgn)
        send(kv.at[x, far], kv.at[x, far], skz.at[6], rkz.at[far], dev(dz=2 * sgn))
        kv_along_x(left)
        kv_along_x(right)

    def distant():
        kv_along_x(kv_here(-3))
        kv_along_x(kv_here(3))
        kv_along_x(kv_here(4))

    def before():
        @pl.when(x >= 1)
        def _():
            def one(zz, c):
                arrive(rk1.at[zz], kv.at[x - 1, zz])
                return c

            lax.fori_loop(0, NZ, one, 0)

    def second(h):
        @pl.when(x >= 1)
        def _():
            unit(1, h)

    def rest_of(h):
        unit(0, h)

    across()
    own_out(0)
    for load in loads[3:5]:
        load.wait()
    row = i * ROWS + lax.broadcasted_iota(jnp.int32, (ROWS, 1), 0)
    starts, ends, at = [], [], jnp.int32(0)
    for d in range(4):
        starts.append(at)
        at = at + doc_ref[0, d] * BLK
        ends.append(at)
    member = [(row >= starts[d]) & (row < ends[d]) for d in range(4)]
    first = jnp.zeros((ROWS, 1), jnp.int32)
    for d in range(4):
        first = jnp.where(member[d], starts[d], first)
    limit = (row // BLK + 1) * BLK

    lane = lax.broadcasted_iota(jnp.int32, (ROWS, ROWS), 1)

    def home(zz):
        return jnp.where((zz <= z) | (x < 2), x, x - 2)

    bases = [home(zz) * NZ * ROWS + zz * ROWS for zz in range(NZ)]
    bases += [(x - 1) * NZ * ROWS + zz * ROWS for zz in range(NZ)]
    bases += [(x - 2) * NZ * ROWS + z * ROWS]
    for n, base in enumerate(bases):
        bias[:, n * ROWS : (n + 1) * ROWS] = jnp.where(
            (lane >= first - base) & (lane < limit - base), 0.0, NEG
        )

    for load in loads[5:]:
        load.wait()

    def unit(b, h):
        def cols(n):
            return pl.ds(pl.multiple_of((2 * h + n) * HEAD, HEAD), HEAD)

        q = jnp.concatenate([q_ref[:, cols(0)], q_ref[:, cols(1)]], axis=0)
        if b == 0:
            spots = [(home(zz), zz) for zz in range(NZ)]
            mask = bias[:, : NZ * ROWS]
        else:
            spots = [(x - 1, zz) for zz in range(NZ)] + [(jnp.maximum(x - 2, 0), z)]
            mask = bias[:, NZ * ROWS :]
        keys = jnp.concatenate([kv[xx, zz, 0] for xx, zz in spots], axis=0)
        vals = jnp.concatenate([kv[xx, zz, 1] for xx, zz in spots], axis=0)
        s = nt_dot(q, keys) * (HEAD ** -0.5 * LOG2E) + jnp.concatenate([mask, mask], axis=0)
        best = jnp.max(s, axis=1, keepdims=True)
        if b == 1:
            old = m_s[h][:, :1]
            best = jnp.maximum(best, old)
        p = jnp.exp2(s - best)
        total = jnp.sum(p, axis=1, keepdims=True)
        summed = jnp.dot(p.astype(jnp.bfloat16), vals, preferred_element_type=jnp.float32)
        if b == 1:
            alpha = jnp.exp2(old - best)
            total = total + alpha * l_s[h][:, :1]
            summed = summed + alpha * acc[h]
        m_s[h] = jnp.broadcast_to(best, (2 * ROWS, HEAD))
        l_s[h] = jnp.broadcast_to(total, (2 * ROWS, HEAD))
        acc[h] = summed

    def finish(h):
        second(h)
        done = (acc[h] / l_s[h]).astype(jnp.bfloat16)
        for n in range(2):
            ab[x, :, (2 * h + n) * HEAD : (2 * h + n + 1) * HEAD] = done[n * ROWS : (n + 1) * ROWS]
        piece = ab.at[x, :, pl.ds(2 * h * HEAD, 2 * HEAD)]
        for n, dx in enumerate((1, -1)):
            send(piece, piece, sa.at[h, n], ra.at[h, n], dev(dx=dx))

    def all_weights(cl):
        def one(zz, c):
            arrive(rwd.at[cl, zz], w.at[cl, 1 - sec, zz])
            return c

        lax.fori_loop(0, NZ, one, 0)

    def project(j):
        dx = (0, -1, 1, 0)[j]
        cl = j // 3
        xx = (x + dx + NX) % NX
        if dx:
            for h in range(4):
                arrive(ra.at[h, j - 1], ab.at[xx, :, pl.ds(2 * h * HEAD, 2 * HEAD)])
        for s2 in range(2):
            o = nt_dot(ab[xx], w[cl, s2].reshape(512, 1024))
            ob[j, s2] = o.astype(jnp.bfloat16)
            to = 2 * s2 + ((x + 2 * cl) % NX) // 2
            lo = x % 2
            if dx:
                send(ob.at[j, s2], rb.at[lo, t], so.at[j, s2], ro.at[lo, t], (sec, xx * NZ + z, to))
            else:
                @pl.when(to == t)
                def _():
                    pltpu.make_async_copy(ob.at[j, s2], rb.at[lo, t], ro.at[lo, t]).start()

                @pl.when(to != t)
                def _():
                    send(ob.at[j, s2], rb.at[lo, t], so.at[j, s2], ro.at[lo, t], (sec, i, to))

    near()
    old_first()
    ring(0,1)
    own_out(1)
    distant()
    old_second()
    ring(0,2)
    ring(1,1)
    old_last()
    rest_of(0)
    rest_of(1)
    ring(0,3)
    rest_of(2)
    rest_of(3)
    ring(1,2)
    before()
    finish(0)
    finish(1)
    ring(0,4)
    finish(2)
    finish(3)
    ring(1,3)
    all_weights(0)
    project(0)
    ring(1,4)
    project(1)
    project(2)
    all_weights(1)
    project(3)
    squares = jnp.zeros((ROWS, 128), jnp.float32)
    for lo in range(2):
        for ts in range(NT):
            arrive(ro.at[lo, ts], rb.at[lo, ts])
        for c in range(4):
            cols = slice(c * 128, c * 128 + 128)
            wide = slice(lo * 512 + c * 128, lo * 512 + c * 128 + 128)
            h = res_ref[:, wide].astype(jnp.float32)
            for ts in range(NT):
                h = h + rb[lo, ts, :, cols].astype(jnp.float32)
            hid[:, wide] = h
            squares = squares + h * h
    column = jnp.broadcast_to(jnp.sum(squares, axis=1, keepdims=True), (ROWS, 128))
    sq[t] = jnp.transpose(column)[:8]
    for n, d in enumerate((1, 2, 3)):
        send(sq.at[t], sq.at[t], ss.at[n], rs.at[n], (sec, i, (t + d) % NT))
    gains = []
    for d in range(4):
        gains.append(gain_ref[...] * (1.0 + shift_ref[pl.ds(noise_ref[0, d], 1), :]))
    for n in range(7):
        arrive(skz.at[n], kv.at[0, 0])

    def drain(zz, c):
        for cl in range(2):
            arrive(swd.at[cl, zz], w.at[0, 0, 0])

        @pl.when(x < NX - 1)
        def _():
            arrive(skx1.at[zz], kv.at[0, 0])

        return c

    lax.fori_loop(0, NZ, drain, 0)
    arrive(swx.at[0], w.at[0, 0, 0])
    for cl in range(2):
        for k in range(4):
            arrive(swf.at[cl, k], w.at[0, 0, 0])
        for k in range(3):
            arrive(swb.at[cl, k], w.at[0, 0, 0])
    for h in range(4):
        for n in range(2):
            arrive(sa.at[h, n], ab.at[0, :, pl.ds(0, 2 * HEAD)])
    for s2 in range(2):
        for cl in range(2):
            @pl.when(2 * s2 + ((x + 2 * cl) % NX) // 2 != t)
            def _():
                arrive(so.at[3 * cl, s2], rb.at[0, 0])

        for j in (1, 2):
            arrive(so.at[j, s2], rb.at[0, 0])

    @pl.when(x < NX - 2)
    def _():
        arrive(sxx.at[0], kv.at[0, 0])

    def sent(cond, n):
        @pl.when(cond)
        def _():
            arrive(sk2.at[n], kv.at[0, 0])

    sent(need(z, 1), 0)
    sent(need(z, -1), 1)
    sent(by_two(z, 1), 2)
    sent(by_two(z, -1), 3)
    sent(need(zmod(z - 2), 3), 4)
    sent(need(zmod(z + 2), -3), 5)
    sent(need(zmod(z - 2 * sgn), 4), 6)

    for n, d in enumerate((1, 2, 3)):
        arrive(rs.at[n], sq.at[(t - d + NT) % NT])
    for n in range(3):
        arrive(ss.at[n], sq.at[0])
    whole = sq[0] + sq[1] + sq[2] + sq[3]
    inverse = jnp.transpose(jnp.broadcast_to(lax.rsqrt(whole[:1] / D + 1e-6), (ROWS, 128)))
    for c in range(8):
        cols = slice(c * 128, c * 128 + 128)
        g = jnp.broadcast_to(gains[0][:, cols], (ROWS, 128))
        for d in range(1, 4):
            g = jnp.where(member[d], gains[d][:, cols], g)
        out_ref[:, cols] = (hid[:, cols] * inverse * g).astype(jnp.bfloat16)


def on_device(queries, keys, values, residual, out_weight, norm_gain, level_shift, doc_lengths, noise_level):
    bf, f32, sem = jnp.bfloat16, jnp.float32, pltpu.SemaphoreType.DMA
    vm = pl.BlockSpec(memory_space=pltpu.VMEM)
    hbm = pl.BlockSpec(memory_space=pltpu.MemorySpace.HBM)
    return pl.pallas_call(
        kernel,
        out_shape=jax.ShapeDtypeStruct((ROWS, 1024), bf),
        in_specs=[hbm] * 9,
        out_specs=vm,
        scratch_shapes=[
            pltpu.SMEM((1, 4), jnp.int32),
            pltpu.SMEM((1, 4), jnp.int32),
            pltpu.VMEM((ROWS, 1024), bf),
            pltpu.VMEM((ROWS, 1024), bf),
            pltpu.VMEM((1, 1024), f32),
            pltpu.VMEM((8, 1024), f32),
            pltpu.VMEM((NX, NZ, 2, ROWS, HEAD), bf),
            pltpu.VMEM((2, 2, NZ, 64, 1024), bf),
            pltpu.VMEM((ROWS, 17 * ROWS), f32),
            pltpu.VMEM((4, 2 * ROWS, HEAD), f32),
            pltpu.VMEM((4, 2 * ROWS, HEAD), f32),
            pltpu.VMEM((4, 2 * ROWS, HEAD), f32),
            pltpu.VMEM((NX, ROWS, 1024), bf),
            pltpu.VMEM((4, 2, ROWS, 512), bf),
            pltpu.VMEM((2, NT, ROWS, 512), bf),
            pltpu.VMEM((ROWS, 1024), f32),
            pltpu.VMEM((NT, 8, 128), f32),
            sem((9,)), sem((7,)), sem((NZ,)), sem((1,)), sem((7,)),
            sem((1,)), sem((2, 4)), sem((2, 3)), sem((2, NZ)), sem((4, 2)), sem((4, 2)), sem((3,)),
            sem((NZ,)), sem((NZ,)), sem((NZ,)),
            sem((1,)), sem((2, NZ)), sem((2, NZ)), sem((4, 2)), sem((2, NT)), sem((3,)),
        ],
        compiler_params=pltpu.CompilerParams(
            collective_id=0, has_side_effects=True, vmem_limit_bytes=64 << 20
        ),
    )(
        doc_lengths, noise_level, queries, keys, values, residual, out_weight.T,
        norm_gain.reshape(1, 1024), level_shift,
    )


def solution(mesh):
    placed = (
        P(("section", "srv"), "tp"),
        P(("section", "srv"), "tp"),
        P(("section", "srv"), "tp"),
        P(("section", "srv"), "tp"),
        P("tp", ("section", "srv")),
        P("tp"),
        P(None, "tp"),
        P("section", None),
        P("section", None),
    )
    return jax.shard_map(
        on_device,
        mesh=mesh,
        in_specs=placed,
        out_specs=P(("section", "srv"), "tp"),
        check_vma=False,
    )
```

```python
import functools

import jax
import jax.numpy as jnp
from jax import lax
from jax.experimental import pallas as pl
from jax.experimental.pallas import tpu as pltpu
from jax.sharding import PartitionSpec as P

D = 4096
HEAD = 128
BLK = 16
ROWS = 128
NX = 4
NZ = 8
NT = 4
MESH = pl.DeviceIdType.MESH
NEG = -1e30
LOG2E = 1.4426950408889634


def arrive(sem, ref):
    pltpu.make_async_copy(ref, ref, sem).wait()


def nt_dot(a, b):
    return lax.dot_general(a, b, (((1,), (1,)), ((), ())), preferred_element_type=jnp.float32)


def kernel(
    doc_in, noise_in, q_in, k_in, v_in, res_in, wt_in, gain_in, shift_in, out_ref,
    doc_ref, noise_ref, q_ref, res_ref, gain_ref, shift_ref,
    kv, w, bias, m_s, l_s, acc, ab, ob, rb, hid, sq,
    sin, skz, skx1, sxx, sk2, swx, swf, swb, swd, sa, so, ss,
    rkz, rk1, rk2, rwx, rw, rwd, ra, ro, rs,
):
    sec = lax.axis_index("section")
    i = lax.axis_index("srv")
    t = lax.axis_index("tp")
    x = i // NZ
    z = i % NZ
    sgn = 1 - 2 * sec

    def dev(dx=0, dz=0):
        return (sec, ((x + dx + NX) % NX) * NZ + (z + dz + 2 * NZ) % NZ, t)

    def zmod(a):
        return (a + 2 * NZ) % NZ

    def send(src, dst, s, r, to):
        pltpu.make_async_remote_copy(
            src_ref=src, dst_ref=dst, send_sem=s, recv_sem=r, device_id=to, device_id_type=MESH
        ).start()

    peers = [dev(dz=1), dev(dz=-1), dev(dz=2), dev(dz=-2), (1 - sec, i, t)]
    peers.append(dev(dx=2))
    for dx in (-1, 0, 1):
        for d in range(NT):
            if dx or d:
                peers.append((sec, ((x + dx + NX) % NX) * NZ + z, (t + d) % NT))
    barrier = pltpu.get_barrier_semaphore()
    for peer in peers:
        pl.semaphore_signal(barrier, inc=1, device_id=peer, device_id_type=MESH)
    loads = [
        pltpu.make_async_copy(src, dst, sin.at[n])
        for n, (src, dst) in enumerate((
            (k_in, kv.at[x, z, 0]),
            (v_in, kv.at[x, z, 1]),
            (wt_in, w.at[0, sec, z]),
            (doc_in, doc_ref),
            (noise_in, noise_ref),
            (q_in, q_ref),
            (gain_in, gain_ref),
            (shift_in, shift_ref),
            (res_in, res_ref),
        ))
    ]
    for load in loads:
        load.start()
    for load in loads[:3]:
        load.wait()
    pl.semaphore_wait(barrier, len(peers))

    def kv_along_x(zz):
        @pl.when(x < NX - 1)
        def _():
            send(kv.at[x, zz], kv.at[x, zz], skx1.at[zz], rk1.at[zz], dev(dx=1))

    def when_send(cond, zz, n, dz):
        @pl.when(cond)
        def _():
            send(kv.at[x - 2, zz], kv.at[x - 2, zz], sk2.at[n], rk2.at[zz], dev(dz=dz))

    def when_here(cond, zz):
        @pl.when(cond)
        def _():
            arrive(rk2.at[zz], kv.at[x - 2, zz])

    def need(zz, d):
        return (x >= 2) & (zmod(zz + d) < zz)

    def by_two(zz, side):
        return need(zz, 2 * side) | need(zz, 3 * side) | (need(zz, 4) & (sgn == side))

    def old_first():
        when_here(x >= 2, z)
        when_send(need(z, 1), z, 0, 1)
        when_send(need(z, -1), z, 1, -1)
        when_send(by_two(z, 1), z, 2, 2)
        when_send(by_two(z, -1), z, 3, -2)

    def old_second():
        for side in (1, -1):
            zz = zmod(z - 2 * side)
            when_here(by_two(zz, side), zz)
            when_send(need(zz, 3 * side), zz, 4 + (1 - side) // 2, side)
        zz = zmod(z - 2 * sgn)
        when_send(need(zz, 4), zz, 6, 2 * sgn)

    def old_last():
        for d in (1, -1, 3, -3, 4):
            zz = zmod(z - d)
            when_here(need(zz, d), zz)

    for n, dz in enumerate((1, -1, 2, -2)):
        send(kv.at[x, z], kv.at[x, z], skz.at[n], rkz.at[z], dev(dz=dz))
    kv_along_x(z)

    @pl.when(x < NX - 2)
    def _():
        send(kv.at[x, z], kv.at[x, z], sxx.at[0], rk2.at[z], dev(dx=2))

    def kv_here(dz):
        zz = zmod(z + dz)
        arrive(rkz.at[zz], kv.at[x, zz])
        return zz

    def across():
        send(w.at[0, sec, z], w.at[1, sec, z], swx.at[0], rwx.at[0], dev(dx=2))

    def own_out(cl):
        piece = w.at[cl, sec, z]
        if cl:
            arrive(rwx.at[0], piece)
        send(piece, piece, swf.at[cl, 0], rw.at[cl, z], dev(dz=sgn))
        send(piece, piece, swb.at[cl, 0], rw.at[cl, z], dev(dz=-sgn))
        send(piece, piece, swd.at[cl, z], rwd.at[cl, z], (1 - sec, i, t))

    def ring(cl, k):
        zf = zmod(z - sgn * k)
        piece = w.at[cl, sec, zf]
        arrive(rw.at[cl, zf], piece)
        if k <= 3:
            send(piece, piece, swf.at[cl, k], rw.at[cl, zf], dev(dz=sgn))
        send(piece, piece, swd.at[cl, zf], rwd.at[cl, zf], (1 - sec, i, t))
        if k <= 3:
            zb = zmod(z + sgn * k)
            piece = w.at[cl, sec, zb]
            arrive(rw.at[cl, zb], piece)
            if k <= 2:
                send(piece, piece, swb.at[cl, k], rw.at[cl, zb], dev(dz=-sgn))
            send(piece, piece, swd.at[cl, zb], rwd.at[cl, zb], (1 - sec, i, t))

    def near():
        kv_along_x(kv_here(-1))
        kv_along_x(kv_here(1))
        left = kv_here(-2)
        send(kv.at[x, left], kv.at[x, left], skz.at[4], rkz.at[left], dev(dz=1))
        right = kv_here(2)
        send(kv.at[x, right], kv.at[x, right], skz.at[5], rkz.at[right], dev(dz=-1))
        far = zmod(z - 2 * sgn)
        send(kv.at[x, far], kv.at[x, far], skz.at[6], rkz.at[far], dev(dz=2 * sgn))
        kv_along_x(left)
        kv_along_x(right)

    def distant():
        kv_along_x(kv_here(-3))
        kv_along_x(kv_here(3))
        kv_along_x(kv_here(4))

    def before():
        @pl.when(x >= 1)
        def _():
            def one(zz, c):
                arrive(rk1.at[zz], kv.at[x - 1, zz])
                return c

            lax.fori_loop(0, NZ, one, 0)

    def second(h):
        @pl.when(x >= 1)
        def _():
            unit(1, h)

    def rest_of(h):
        unit(0, h)

    own_out(0)
    for load in loads[3:5]:
        load.wait()
    row = i * ROWS + lax.broadcasted_iota(jnp.int32, (ROWS, 1), 0)
    starts, ends, at = [], [], jnp.int32(0)
    for d in range(4):
        starts.append(at)
        at = at + doc_ref[0, d] * BLK
        ends.append(at)
    member = [(row >= starts[d]) & (row < ends[d]) for d in range(4)]
    first = jnp.zeros((ROWS, 1), jnp.int32)
    for d in range(4):
        first = jnp.where(member[d], starts[d], first)
    limit = (row // BLK + 1) * BLK

    lane = lax.broadcasted_iota(jnp.int32, (ROWS, ROWS), 1)

    def home(zz):
        return jnp.where((zz <= z) | (x < 2), x, x - 2)

    bases = [home(zz) * NZ * ROWS + zz * ROWS for zz in range(NZ)]
    bases += [(x - 1) * NZ * ROWS + zz * ROWS for zz in range(NZ)]
    bases += [(x - 2) * NZ * ROWS + z * ROWS]
    for n, base in enumerate(bases):
        bias[:, n * ROWS : (n + 1) * ROWS] = jnp.where(
            (lane >= first - base) & (lane < limit - base), 0.0, NEG
        )

    for load in loads[5:]:
        load.wait()

    def unit(b, h):
        def cols(n):
            return pl.ds(pl.multiple_of((2 * h + n) * HEAD, HEAD), HEAD)

        q = jnp.concatenate([q_ref[:, cols(0)], q_ref[:, cols(1)]], axis=0)
        if b == 0:
            spots = [(home(zz), zz) for zz in range(NZ)]
            mask = bias[:, : NZ * ROWS]
        else:
            spots = [(x - 1, zz) for zz in range(NZ)] + [(jnp.maximum(x - 2, 0), z)]
            mask = bias[:, NZ * ROWS :]
        keys = jnp.concatenate([kv[xx, zz, 0] for xx, zz in spots], axis=0)
        vals = jnp.concatenate([kv[xx, zz, 1] for xx, zz in spots], axis=0)
        s = nt_dot(q, keys) * (HEAD ** -0.5 * LOG2E) + jnp.concatenate([mask, mask], axis=0)
        best = jnp.max(s, axis=1, keepdims=True)
        if b == 1:
            old = m_s[h][:, :1]
            best = jnp.maximum(best, old)
        p = jnp.exp2(s - best)
        total = jnp.sum(p, axis=1, keepdims=True)
        summed = jnp.dot(p.astype(jnp.bfloat16), vals, preferred_element_type=jnp.float32)
        if b == 1:
            alpha = jnp.exp2(old - best)
            total = total + alpha * l_s[h][:, :1]
            summed = summed + alpha * acc[h]
        m_s[h] = jnp.broadcast_to(best, (2 * ROWS, HEAD))
        l_s[h] = jnp.broadcast_to(total, (2 * ROWS, HEAD))
        acc[h] = summed

    def finish(h):
        second(h)
        done = (acc[h] / l_s[h]).astype(jnp.bfloat16)
        for n in range(2):
            ab[x, :, (2 * h + n) * HEAD : (2 * h + n + 1) * HEAD] = done[n * ROWS : (n + 1) * ROWS]
        piece = ab.at[x, :, pl.ds(2 * h * HEAD, 2 * HEAD)]
        for n, dx in enumerate((1, -1)):
            send(piece, piece, sa.at[h, n], ra.at[h, n], dev(dx=dx))

    def all_weights(cl):
        def one(zz, c):
            arrive(rwd.at[cl, zz], w.at[cl, 1 - sec, zz])
            return c

        lax.fori_loop(0, NZ, one, 0)

    def project(j):
        dx = (0, -1, 1, 0)[j]
        cl = j // 3
        xx = (x + dx + NX) % NX
        if dx:
            for h in range(4):
                arrive(ra.at[h, j - 1], ab.at[xx, :, pl.ds(2 * h * HEAD, 2 * HEAD)])
        for s2 in range(2):
            o = nt_dot(ab[xx], w[cl, s2].reshape(512, 1024))
            ob[j, s2] = o.astype(jnp.bfloat16)
            to = 2 * s2 + ((x + 2 * cl) % NX) // 2
            lo = x % 2
            if dx:
                send(ob.at[j, s2], rb.at[lo, t], so.at[j, s2], ro.at[lo, t], (sec, xx * NZ + z, to))
            else:
                @pl.when(to == t)
                def _():
                    pltpu.make_async_copy(ob.at[j, s2], rb.at[lo, t], ro.at[lo, t]).start()

                @pl.when(to != t)
                def _():
                    send(ob.at[j, s2], rb.at[lo, t], so.at[j, s2], ro.at[lo, t], (sec, i, to))

    near()
    old_first()
    ring(0,1)
    distant()
    across()
    old_second()
    ring(0,2)
    own_out(1)
    old_last()
    rest_of(0)
    rest_of(1)
    ring(0,3)
    rest_of(2)
    rest_of(3)
    ring(1,1)
    before()
    finish(0)
    finish(1)
    ring(0,4)
    finish(2)
    finish(3)
    ring(1,2)
    all_weights(0)
    project(0)
    ring(1,3)
    project(1)
    project(2)
    ring(1,4)
    all_weights(1)
    project(3)
    squares = jnp.zeros((ROWS, 128), jnp.float32)
    for lo in range(2):
        for ts in range(NT):
            arrive(ro.at[lo, ts], rb.at[lo, ts])
        for c in range(4):
            cols = slice(c * 128, c * 128 + 128)
            wide = slice(lo * 512 + c * 128, lo * 512 + c * 128 + 128)
            h = res_ref[:, wide].astype(jnp.float32)
            for ts in range(NT):
                h = h + rb[lo, ts, :, cols].astype(jnp.float32)
            hid[:, wide] = h
            squares = squares + h * h
    column = jnp.broadcast_to(jnp.sum(squares, axis=1, keepdims=True), (ROWS, 128))
    sq[t] = jnp.transpose(column)[:8]
    for n, d in enumerate((1, 2, 3)):
        send(sq.at[t], sq.at[t], ss.at[n], rs.at[n], (sec, i, (t + d) % NT))
    gains = []
    for d in range(4):
        gains.append(gain_ref[...] * (1.0 + shift_ref[pl.ds(noise_ref[0, d], 1), :]))
    for n in range(7):
        arrive(skz.at[n], kv.at[0, 0])

    def drain(zz, c):
        for cl in range(2):
            arrive(swd.at[cl, zz], w.at[0, 0, 0])

        @pl.when(x < NX - 1)
        def _():
            arrive(skx1.at[zz], kv.at[0, 0])

        return c

    lax.fori_loop(0, NZ, drain, 0)
    arrive(swx.at[0], w.at[0, 0, 0])
    for cl in range(2):
        for k in range(4):
            arrive(swf.at[cl, k], w.at[0, 0, 0])
        for k in range(3):
            arrive(swb.at[cl, k], w.at[0, 0, 0])
    for h in range(4):
        for n in range(2):
            arrive(sa.at[h, n], ab.at[0, :, pl.ds(0, 2 * HEAD)])
    for s2 in range(2):
        for cl in range(2):
            @pl.when(2 * s2 + ((x + 2 * cl) % NX) // 2 != t)
            def _():
                arrive(so.at[3 * cl, s2], rb.at[0, 0])

        for j in (1, 2):
            arrive(so.at[j, s2], rb.at[0, 0])

    @pl.when(x < NX - 2)
    def _():
        arrive(sxx.at[0], kv.at[0, 0])

    def sent(cond, n):
        @pl.when(cond)
        def _():
            arrive(sk2.at[n], kv.at[0, 0])

    sent(need(z, 1), 0)
    sent(need(z, -1), 1)
    sent(by_two(z, 1), 2)
    sent(by_two(z, -1), 3)
    sent(need(zmod(z - 2), 3), 4)
    sent(need(zmod(z + 2), -3), 5)
    sent(need(zmod(z - 2 * sgn), 4), 6)

    for n, d in enumerate((1, 2, 3)):
        arrive(rs.at[n], sq.at[(t - d + NT) % NT])
    for n in range(3):
        arrive(ss.at[n], sq.at[0])
    whole = sq[0] + sq[1] + sq[2] + sq[3]
    inverse = jnp.transpose(jnp.broadcast_to(lax.rsqrt(whole[:1] / D + 1e-6), (ROWS, 128)))
    for c in range(8):
        cols = slice(c * 128, c * 128 + 128)
        g = jnp.broadcast_to(gains[0][:, cols], (ROWS, 128))
        for d in range(1, 4):
            g = jnp.where(member[d], gains[d][:, cols], g)
        out_ref[:, cols] = (hid[:, cols] * inverse * g).astype(jnp.bfloat16)


def on_device(queries, keys, values, residual, out_weight, norm_gain, level_shift, doc_lengths, noise_level):
    bf, f32, sem = jnp.bfloat16, jnp.float32, pltpu.SemaphoreType.DMA
    vm = pl.BlockSpec(memory_space=pltpu.VMEM)
    hbm = pl.BlockSpec(memory_space=pltpu.MemorySpace.HBM)
    return pl.pallas_call(
        kernel,
        out_shape=jax.ShapeDtypeStruct((ROWS, 1024), bf),
        in_specs=[hbm] * 9,
        out_specs=vm,
        scratch_shapes=[
            pltpu.SMEM((1, 4), jnp.int32),
            pltpu.SMEM((1, 4), jnp.int32),
            pltpu.VMEM((ROWS, 1024), bf),
            pltpu.VMEM((ROWS, 1024), bf),
            pltpu.VMEM((1, 1024), f32),
            pltpu.VMEM((8, 1024), f32),
            pltpu.VMEM((NX, NZ, 2, ROWS, HEAD), bf),
            pltpu.VMEM((2, 2, NZ, 64, 1024), bf),
            pltpu.VMEM((ROWS, 17 * ROWS), f32),
            pltpu.VMEM((4, 2 * ROWS, HEAD), f32),
            pltpu.VMEM((4, 2 * ROWS, HEAD), f32),
            pltpu.VMEM((4, 2 * ROWS, HEAD), f32),
            pltpu.VMEM((NX, ROWS, 1024), bf),
            pltpu.VMEM((4, 2, ROWS, 512), bf),
            pltpu.VMEM((2, NT, ROWS, 512), bf),
            pltpu.VMEM((ROWS, 1024), f32),
            pltpu.VMEM((NT, 8, 128), f32),
            sem((9,)), sem((7,)), sem((NZ,)), sem((1,)), sem((7,)),
            sem((1,)), sem((2, 4)), sem((2, 3)), sem((2, NZ)), sem((4, 2)), sem((4, 2)), sem((3,)),
            sem((NZ,)), sem((NZ,)), sem((NZ,)),
            sem((1,)), sem((2, NZ)), sem((2, NZ)), sem((4, 2)), sem((2, NT)), sem((3,)),
        ],
        compiler_params=pltpu.CompilerParams(
            collective_id=0, has_side_effects=True, vmem_limit_bytes=64 << 20
        ),
    )(
        doc_lengths, noise_level, queries, keys, values, residual, out_weight.T,
        norm_gain.reshape(1, 1024), level_shift,
    )


def solution(mesh):
    placed = (
        P(("section", "srv"), "tp"),
        P(("section", "srv"), "tp"),
        P(("section", "srv"), "tp"),
        P(("section", "srv"), "tp"),
        P("tp", ("section", "srv")),
        P("tp"),
        P(None, "tp"),
        P("section", None),
        P("section", None),
    )
    return jax.shard_map(
        on_device,
        mesh=mesh,
        in_specs=placed,
        out_specs=P(("section", "srv"), "tp"),
        check_vma=False,
    )
```

```python
import functools

import jax
import jax.numpy as jnp
from jax import lax
from jax.experimental import pallas as pl
from jax.experimental.pallas import tpu as pltpu
from jax.sharding import PartitionSpec as P

D = 4096
HEAD = 128
BLK = 16
ROWS = 128
NX = 4
NZ = 8
NT = 4
MESH = pl.DeviceIdType.MESH
NEG = -1e30
LOG2E = 1.4426950408889634


def arrive(sem, ref):
    pltpu.make_async_copy(ref, ref, sem).wait()


def nt_dot(a, b):
    return lax.dot_general(a, b, (((1,), (1,)), ((), ())), preferred_element_type=jnp.float32)


def kernel(
    doc_in, noise_in, q_in, k_in, v_in, res_in, wt_in, gain_in, shift_in, out_ref,
    doc_ref, noise_ref, q_ref, res_ref, gain_ref, shift_ref,
    kv, w, bias, m_s, l_s, acc, ab, ob, rb, hid, sq,
    sin, skz, skx1, sxx, sk2, swx, swf, swb, swd, sa, so, ss,
    rkz, rk1, rk2, rwx, rw, rwd, ra, ro, rs,
):
    sec = lax.axis_index("section")
    i = lax.axis_index("srv")
    t = lax.axis_index("tp")
    x = i // NZ
    z = i % NZ
    sgn = 1 - 2 * sec

    def dev(dx=0, dz=0):
        return (sec, ((x + dx + NX) % NX) * NZ + (z + dz + 2 * NZ) % NZ, t)

    def zmod(a):
        return (a + 2 * NZ) % NZ

    def send(src, dst, s, r, to):
        pltpu.make_async_remote_copy(
            src_ref=src, dst_ref=dst, send_sem=s, recv_sem=r, device_id=to, device_id_type=MESH
        ).start()

    peers = [dev(dz=1), dev(dz=-1), dev(dz=2), dev(dz=-2), (1 - sec, i, t)]
    peers.append(dev(dx=2))
    for dx in (-1, 0, 1):
        for d in range(NT):
            if dx or d:
                peers.append((sec, ((x + dx + NX) % NX) * NZ + z, (t + d) % NT))
    barrier = pltpu.get_barrier_semaphore()
    for peer in peers:
        pl.semaphore_signal(barrier, inc=1, device_id=peer, device_id_type=MESH)
    loads = [
        pltpu.make_async_copy(src, dst, sin.at[n])
        for n, (src, dst) in enumerate((
            (k_in, kv.at[x, z, 0]),
            (v_in, kv.at[x, z, 1]),
            (wt_in, w.at[0, sec, z]),
            (doc_in, doc_ref),
            (noise_in, noise_ref),
            (q_in, q_ref),
            (gain_in, gain_ref),
            (shift_in, shift_ref),
            (res_in, res_ref),
        ))
    ]
    for load in loads:
        load.start()
    for load in loads[:3]:
        load.wait()
    pl.semaphore_wait(barrier, len(peers))

    def kv_along_x(zz):
        @pl.when(x < NX - 1)
        def _():
            send(kv.at[x, zz], kv.at[x, zz], skx1.at[zz], rk1.at[zz], dev(dx=1))

    def when_send(cond, zz, n, dz):
        @pl.when(cond)
        def _():
            send(kv.at[x - 2, zz], kv.at[x - 2, zz], sk2.at[n], rk2.at[zz], dev(dz=dz))

    def when_here(cond, zz):
        @pl.when(cond)
        def _():
            arrive(rk2.at[zz], kv.at[x - 2, zz])

    def need(zz, d):
        return (x >= 2) & (zmod(zz + d) < zz)

    def by_two(zz, side):
        return need(zz, 2 * side) | need(zz, 3 * side) | (need(zz, 4) & (sgn == side))

    def old_first():
        when_here(x >= 2, z)
        when_send(need(z, 1), z, 0, 1)
        when_send(need(z, -1), z, 1, -1)
        when_send(by_two(z, 1), z, 2, 2)
        when_send(by_two(z, -1), z, 3, -2)

    def old_second():
        for side in (1, -1):
            zz = zmod(z - 2 * side)
            when_here(by_two(zz, side), zz)
            when_send(need(zz, 3 * side), zz, 4 + (1 - side) // 2, side)
        zz = zmod(z - 2 * sgn)
        when_send(need(zz, 4), zz, 6, 2 * sgn)

    def old_last():
        for d in (1, -1, 3, -3, 4):
            zz = zmod(z - d)
            when_here(need(zz, d), zz)

    for n, dz in enumerate((1, -1, 2, -2)):
        send(kv.at[x, z], kv.at[x, z], skz.at[n], rkz.at[z], dev(dz=dz))
    kv_along_x(z)

    @pl.when(x < NX - 2)
    def _():
        send(kv.at[x, z], kv.at[x, z], sxx.at[0], rk2.at[z], dev(dx=2))

    def kv_here(dz):
        zz = zmod(z + dz)
        arrive(rkz.at[zz], kv.at[x, zz])
        return zz

    def across():
        send(w.at[0, sec, z], w.at[1, sec, z], swx.at[0], rwx.at[0], dev(dx=2))

    def own_out(cl):
        piece = w.at[cl, sec, z]
        if cl:
            arrive(rwx.at[0], piece)
        send(piece, piece, swf.at[cl, 0], rw.at[cl, z], dev(dz=sgn))
        send(piece, piece, swb.at[cl, 0], rw.at[cl, z], dev(dz=-sgn))
        send(piece, piece, swd.at[cl, z], rwd.at[cl, z], (1 - sec, i, t))

    def ring(cl, k):
        zf = zmod(z - sgn * k)
        piece = w.at[cl, sec, zf]
        arrive(rw.at[cl, zf], piece)
        if k <= 3:
            send(piece, piece, swf.at[cl, k], rw.at[cl, zf], dev(dz=sgn))
        send(piece, piece, swd.at[cl, zf], rwd.at[cl, zf], (1 - sec, i, t))
        if k <= 3:
            zb = zmod(z + sgn * k)
            piece = w.at[cl, sec, zb]
            arrive(rw.at[cl, zb], piece)
            if k <= 2:
                send(piece, piece, swb.at[cl, k], rw.at[cl, zb], dev(dz=-sgn))
            send(piece, piece, swd.at[cl, zb], rwd.at[cl, zb], (1 - sec, i, t))

    def near():
        kv_along_x(kv_here(-1))
        kv_along_x(kv_here(1))
        left = kv_here(-2)
        send(kv.at[x, left], kv.at[x, left], skz.at[4], rkz.at[left], dev(dz=1))
        right = kv_here(2)
        send(kv.at[x, right], kv.at[x, right], skz.at[5], rkz.at[right], dev(dz=-1))
        far = zmod(z - 2 * sgn)
        send(kv.at[x, far], kv.at[x, far], skz.at[6], rkz.at[far], dev(dz=2 * sgn))
        kv_along_x(left)
        kv_along_x(right)

    def distant():
        kv_along_x(kv_here(-3))
        kv_along_x(kv_here(3))
        kv_along_x(kv_here(4))

    def before():
        @pl.when(x >= 1)
        def _():
            def one(zz, c):
                arrive(rk1.at[zz], kv.at[x - 1, zz])
                return c

            lax.fori_loop(0, NZ, one, 0)

    def second(h):
        @pl.when(x >= 1)
        def _():
            unit(1, h)

    def rest_of(h):
        unit(0, h)

    own_out(0)
    for load in loads[3:5]:
        load.wait()
    row = i * ROWS + lax.broadcasted_iota(jnp.int32, (ROWS, 1), 0)
    starts, ends, at = [], [], jnp.int32(0)
    for d in range(4):
        starts.append(at)
        at = at + doc_ref[0, d] * BLK
        ends.append(at)
    member = [(row >= starts[d]) & (row < ends[d]) for d in range(4)]
    first = jnp.zeros((ROWS, 1), jnp.int32)
    for d in range(4):
        first = jnp.where(member[d], starts[d], first)
    limit = (row // BLK + 1) * BLK

    lane = lax.broadcasted_iota(jnp.int32, (ROWS, ROWS), 1)

    def home(zz):
        return jnp.where((zz <= z) | (x < 2), x, x - 2)

    bases = [home(zz) * NZ * ROWS + zz * ROWS for zz in range(NZ)]
    bases += [(x - 1) * NZ * ROWS + zz * ROWS for zz in range(NZ)]
    bases += [(x - 2) * NZ * ROWS + z * ROWS]
    for n, base in enumerate(bases):
        bias[:, n * ROWS : (n + 1) * ROWS] = jnp.where(
            (lane >= first - base) & (lane < limit - base), 0.0, NEG
        )

    for load in loads[5:]:
        load.wait()

    def unit(b, h):
        def cols(n):
            return pl.ds(pl.multiple_of((2 * h + n) * HEAD, HEAD), HEAD)

        q = jnp.concatenate([q_ref[:, cols(0)], q_ref[:, cols(1)]], axis=0)
        if b == 0:
            spots = [(home(zz), zz) for zz in range(NZ)]
            mask = bias[:, : NZ * ROWS]
        else:
            spots = [(x - 1, zz) for zz in range(NZ)] + [(jnp.maximum(x - 2, 0), z)]
            mask = bias[:, NZ * ROWS :]
        keys = jnp.concatenate([kv[xx, zz, 0] for xx, zz in spots], axis=0)
        vals = jnp.concatenate([kv[xx, zz, 1] for xx, zz in spots], axis=0)
        s = nt_dot(q, keys) * (HEAD ** -0.5 * LOG2E) + jnp.concatenate([mask, mask], axis=0)
        best = jnp.max(s, axis=1, keepdims=True)
        if b == 1:
            old = m_s[h][:, :1]
            best = jnp.maximum(best, old)
        p = jnp.exp2(s - best)
        total = jnp.sum(p, axis=1, keepdims=True)
        summed = jnp.dot(p.astype(jnp.bfloat16), vals, preferred_element_type=jnp.float32)
        if b == 1:
            alpha = jnp.exp2(old - best)
            total = total + alpha * l_s[h][:, :1]
            summed = summed + alpha * acc[h]
        m_s[h] = jnp.broadcast_to(best, (2 * ROWS, HEAD))
        l_s[h] = jnp.broadcast_to(total, (2 * ROWS, HEAD))
        acc[h] = summed

    def finish(h):
        second(h)
        done = (acc[h] / l_s[h]).astype(jnp.bfloat16)
        for n in range(2):
            ab[x, :, (2 * h + n) * HEAD : (2 * h + n + 1) * HEAD] = done[n * ROWS : (n + 1) * ROWS]
        piece = ab.at[x, :, pl.ds(2 * h * HEAD, 2 * HEAD)]
        for n, dx in enumerate((1, -1)):
            send(piece, piece, sa.at[h, n], ra.at[h, n], dev(dx=dx))

    def all_weights(cl):
        def one(zz, c):
            arrive(rwd.at[cl, zz], w.at[cl, 1 - sec, zz])
            return c

        lax.fori_loop(0, NZ, one, 0)

    def project(j):
        dx = (0, -1, 1, 0)[j]
        cl = j // 3
        xx = (x + dx + NX) % NX
        if dx:
            for h in range(4):
                arrive(ra.at[h, j - 1], ab.at[xx, :, pl.ds(2 * h * HEAD, 2 * HEAD)])
        for s2 in range(2):
            o = nt_dot(ab[xx], w[cl, s2].reshape(512, 1024))
            ob[j, s2] = o.astype(jnp.bfloat16)
            to = 2 * s2 + ((x + 2 * cl) % NX) // 2
            lo = x % 2
            if dx:
                send(ob.at[j, s2], rb.at[lo, t], so.at[j, s2], ro.at[lo, t], (sec, xx * NZ + z, to))
            else:
                @pl.when(to == t)
                def _():
                    pltpu.make_async_copy(ob.at[j, s2], rb.at[lo, t], ro.at[lo, t]).start()

                @pl.when(to != t)
                def _():
                    send(ob.at[j, s2], rb.at[lo, t], so.at[j, s2], ro.at[lo, t], (sec, i, to))

    near()
    old_first()
    ring(0,1)
    across()
    distant()
    old_second()
    ring(0,2)
    own_out(1)
    old_last()
    rest_of(0)
    rest_of(1)
    ring(0,3)
    rest_of(2)
    rest_of(3)
    ring(1,1)
    before()
    finish(0)
    finish(1)
    ring(0,4)
    finish(2)
    finish(3)
    ring(1,2)
    all_weights(0)
    project(0)
    ring(1,3)
    project(1)
    project(2)
    ring(1,4)
    all_weights(1)
    project(3)
    squares = jnp.zeros((ROWS, 128), jnp.float32)
    for lo in range(2):
        for ts in range(NT):
            arrive(ro.at[lo, ts], rb.at[lo, ts])
        for c in range(4):
            cols = slice(c * 128, c * 128 + 128)
            wide = slice(lo * 512 + c * 128, lo * 512 + c * 128 + 128)
            h = res_ref[:, wide].astype(jnp.float32)
            for ts in range(NT):
                h = h + rb[lo, ts, :, cols].astype(jnp.float32)
            hid[:, wide] = h
            squares = squares + h * h
    column = jnp.broadcast_to(jnp.sum(squares, axis=1, keepdims=True), (ROWS, 128))
    sq[t] = jnp.transpose(column)[:8]
    for n, d in enumerate((1, 2, 3)):
        send(sq.at[t], sq.at[t], ss.at[n], rs.at[n], (sec, i, (t + d) % NT))
    gains = []
    for d in range(4):
        gains.append(gain_ref[...] * (1.0 + shift_ref[pl.ds(noise_ref[0, d], 1), :]))
    for n in range(7):
        arrive(skz.at[n], kv.at[0, 0])

    def drain(zz, c):
        for cl in range(2):
            arrive(swd.at[cl, zz], w.at[0, 0, 0])

        @pl.when(x < NX - 1)
        def _():
            arrive(skx1.at[zz], kv.at[0, 0])

        return c

    lax.fori_loop(0, NZ, drain, 0)
    arrive(swx.at[0], w.at[0, 0, 0])
    for cl in range(2):
        for k in range(4):
            arrive(swf.at[cl, k], w.at[0, 0, 0])
        for k in range(3):
            arrive(swb.at[cl, k], w.at[0, 0, 0])
    for h in range(4):
        for n in range(2):
            arrive(sa.at[h, n], ab.at[0, :, pl.ds(0, 2 * HEAD)])
    for s2 in range(2):
        for cl in range(2):
            @pl.when(2 * s2 + ((x + 2 * cl) % NX) // 2 != t)
            def _():
                arrive(so.at[3 * cl, s2], rb.at[0, 0])

        for j in (1, 2):
            arrive(so.at[j, s2], rb.at[0, 0])

    @pl.when(x < NX - 2)
    def _():
        arrive(sxx.at[0], kv.at[0, 0])

    def sent(cond, n):
        @pl.when(cond)
        def _():
            arrive(sk2.at[n], kv.at[0, 0])

    sent(need(z, 1), 0)
    sent(need(z, -1), 1)
    sent(by_two(z, 1), 2)
    sent(by_two(z, -1), 3)
    sent(need(zmod(z - 2), 3), 4)
    sent(need(zmod(z + 2), -3), 5)
    sent(need(zmod(z - 2 * sgn), 4), 6)

    for n, d in enumerate((1, 2, 3)):
        arrive(rs.at[n], sq.at[(t - d + NT) % NT])
    for n in range(3):
        arrive(ss.at[n], sq.at[0])
    whole = sq[0] + sq[1] + sq[2] + sq[3]
    inverse = jnp.transpose(jnp.broadcast_to(lax.rsqrt(whole[:1] / D + 1e-6), (ROWS, 128)))
    for c in range(8):
        cols = slice(c * 128, c * 128 + 128)
        g = jnp.broadcast_to(gains[0][:, cols], (ROWS, 128))
        for d in range(1, 4):
            g = jnp.where(member[d], gains[d][:, cols], g)
        out_ref[:, cols] = (hid[:, cols] * inverse * g).astype(jnp.bfloat16)


def on_device(queries, keys, values, residual, out_weight, norm_gain, level_shift, doc_lengths, noise_level):
    bf, f32, sem = jnp.bfloat16, jnp.float32, pltpu.SemaphoreType.DMA
    vm = pl.BlockSpec(memory_space=pltpu.VMEM)
    hbm = pl.BlockSpec(memory_space=pltpu.MemorySpace.HBM)
    return pl.pallas_call(
        kernel,
        out_shape=jax.ShapeDtypeStruct((ROWS, 1024), bf),
        in_specs=[hbm] * 9,
        out_specs=vm,
        scratch_shapes=[
            pltpu.SMEM((1, 4), jnp.int32),
            pltpu.SMEM((1, 4), jnp.int32),
            pltpu.VMEM((ROWS, 1024), bf),
            pltpu.VMEM((ROWS, 1024), bf),
            pltpu.VMEM((1, 1024), f32),
            pltpu.VMEM((8, 1024), f32),
            pltpu.VMEM((NX, NZ, 2, ROWS, HEAD), bf),
            pltpu.VMEM((2, 2, NZ, 64, 1024), bf),
            pltpu.VMEM((ROWS, 17 * ROWS), f32),
            pltpu.VMEM((4, 2 * ROWS, HEAD), f32),
            pltpu.VMEM((4, 2 * ROWS, HEAD), f32),
            pltpu.VMEM((4, 2 * ROWS, HEAD), f32),
            pltpu.VMEM((NX, ROWS, 1024), bf),
            pltpu.VMEM((4, 2, ROWS, 512), bf),
            pltpu.VMEM((2, NT, ROWS, 512), bf),
            pltpu.VMEM((ROWS, 1024), f32),
            pltpu.VMEM((NT, 8, 128), f32),
            sem((9,)), sem((7,)), sem((NZ,)), sem((1,)), sem((7,)),
            sem((1,)), sem((2, 4)), sem((2, 3)), sem((2, NZ)), sem((4, 2)), sem((4, 2)), sem((3,)),
            sem((NZ,)), sem((NZ,)), sem((NZ,)),
            sem((1,)), sem((2, NZ)), sem((2, NZ)), sem((4, 2)), sem((2, NT)), sem((3,)),
        ],
        compiler_params=pltpu.CompilerParams(
            collective_id=0, has_side_effects=True, vmem_limit_bytes=64 << 20
        ),
    )(
        doc_lengths, noise_level, queries, keys, values, residual, out_weight.T,
        norm_gain.reshape(1, 1024), level_shift,
    )


def solution(mesh):
    placed = (
        P(("section", "srv"), "tp"),
        P(("section", "srv"), "tp"),
        P(("section", "srv"), "tp"),
        P(("section", "srv"), "tp"),
        P("tp", ("section", "srv")),
        P("tp"),
        P(None, "tp"),
        P("section", None),
        P("section", None),
    )
    return jax.shard_map(
        on_device,
        mesh=mesh,
        in_specs=placed,
        out_specs=P(("section", "srv"), "tp"),
        check_vma=False,
    )
```

```python
import functools

import jax
import jax.numpy as jnp
from jax import lax
from jax.experimental import pallas as pl
from jax.experimental.pallas import tpu as pltpu
from jax.sharding import PartitionSpec as P

D = 4096
HEAD = 128
BLK = 16
ROWS = 128
NX = 4
NZ = 8
NT = 4
MESH = pl.DeviceIdType.MESH
NEG = -1e30
LOG2E = 1.4426950408889634


def arrive(sem, ref):
    pltpu.make_async_copy(ref, ref, sem).wait()


def nt_dot(a, b):
    return lax.dot_general(a, b, (((1,), (1,)), ((), ())), preferred_element_type=jnp.float32)


def kernel(
    doc_in, noise_in, q_in, k_in, v_in, res_in, wt_in, gain_in, shift_in, out_ref,
    doc_ref, noise_ref, q_ref, res_ref, gain_ref, shift_ref,
    kv, w, bias, m_s, l_s, acc, ab, ob, rb, hid, sq,
    sin, skz, skx1, sxx, sk2, swx, swf, swb, swd, sa, so, ss,
    result, sout, rkz, rk1, rk2, rwx, rw, rwd, ra, ro, rs,
):
    sec = lax.axis_index("section")
    i = lax.axis_index("srv")
    t = lax.axis_index("tp")
    x = i // NZ
    z = i % NZ
    sgn = 1 - 2 * sec

    def dev(dx=0, dz=0):
        return (sec, ((x + dx + NX) % NX) * NZ + (z + dz + 2 * NZ) % NZ, t)

    def zmod(a):
        return (a + 2 * NZ) % NZ

    def send(src, dst, s, r, to):
        pltpu.make_async_remote_copy(
            src_ref=src, dst_ref=dst, send_sem=s, recv_sem=r, device_id=to, device_id_type=MESH
        ).start()

    peers = [dev(dz=1), dev(dz=-1), dev(dz=2), dev(dz=-2), (1 - sec, i, t)]
    peers.append(dev(dx=2))
    for dx in (-1, 0, 1):
        for d in range(NT):
            if dx or d:
                peers.append((sec, ((x + dx + NX) % NX) * NZ + z, (t + d) % NT))
    barrier = pltpu.get_barrier_semaphore()
    for peer in peers:
        pl.semaphore_signal(barrier, inc=1, device_id=peer, device_id_type=MESH)
    loads = [
        pltpu.make_async_copy(src, dst, sin.at[n])
        for n, (src, dst) in enumerate((
            (k_in, kv.at[x, z, 0]),
            (v_in, kv.at[x, z, 1]),
            (wt_in, w.at[0, sec, z]),
            (doc_in, doc_ref),
            (noise_in, noise_ref),
            (q_in, q_ref),
            (gain_in, gain_ref),
            (shift_in, shift_ref),
            (res_in, res_ref),
        ))
    ]
    for load in loads:
        load.start()
    for load in loads[:3]:
        load.wait()
    pl.semaphore_wait(barrier, len(peers))

    def kv_along_x(zz):
        @pl.when(x < NX - 1)
        def _():
            send(kv.at[x, zz], kv.at[x, zz], skx1.at[zz], rk1.at[zz], dev(dx=1))

    def when_send(cond, zz, n, dz):
        @pl.when(cond)
        def _():
            send(kv.at[x - 2, zz], kv.at[x - 2, zz], sk2.at[n], rk2.at[zz], dev(dz=dz))

    def when_here(cond, zz):
        @pl.when(cond)
        def _():
            arrive(rk2.at[zz], kv.at[x - 2, zz])

    def need(zz, d):
        return (x >= 2) & (zmod(zz + d) < zz)

    def by_two(zz, side):
        return need(zz, 2 * side) | need(zz, 3 * side) | (need(zz, 4) & (sgn == side))

    def old_first():
        when_here(x >= 2, z)
        when_send(need(z, 1), z, 0, 1)
        when_send(need(z, -1), z, 1, -1)
        when_send(by_two(z, 1), z, 2, 2)
        when_send(by_two(z, -1), z, 3, -2)

    def old_second():
        for side in (1, -1):
            zz = zmod(z - 2 * side)
            when_here(by_two(zz, side), zz)
            when_send(need(zz, 3 * side), zz, 4 + (1 - side) // 2, side)
        zz = zmod(z - 2 * sgn)
        when_send(need(zz, 4), zz, 6, 2 * sgn)

    def old_last():
        for d in (1, -1, 3, -3, 4):
            zz = zmod(z - d)
            when_here(need(zz, d), zz)

    for n, dz in enumerate((1, -1, 2, -2)):
        send(kv.at[x, z], kv.at[x, z], skz.at[n], rkz.at[z], dev(dz=dz))
    kv_along_x(z)

    @pl.when(x < NX - 2)
    def _():
        send(kv.at[x, z], kv.at[x, z], sxx.at[0], rk2.at[z], dev(dx=2))

    def kv_here(dz):
        zz = zmod(z + dz)
        arrive(rkz.at[zz], kv.at[x, zz])
        return zz

    def across():
        send(w.at[0, sec, z], w.at[1, sec, z], swx.at[0], rwx.at[0], dev(dx=2))

    def own_out(cl):
        piece = w.at[cl, sec, z]
        if cl:
            arrive(rwx.at[0], piece)
        send(piece, piece, swf.at[cl, 0], rw.at[cl, z], dev(dz=sgn))
        send(piece, piece, swb.at[cl, 0], rw.at[cl, z], dev(dz=-sgn))
        send(piece, piece, swd.at[cl, z], rwd.at[cl, z], (1 - sec, i, t))

    def ring(cl, k):
        zf = zmod(z - sgn * k)
        piece = w.at[cl, sec, zf]
        arrive(rw.at[cl, zf], piece)
        if k <= 3:
            send(piece, piece, swf.at[cl, k], rw.at[cl, zf], dev(dz=sgn))
        send(piece, piece, swd.at[cl, zf], rwd.at[cl, zf], (1 - sec, i, t))
        if k <= 3:
            zb = zmod(z + sgn * k)
            piece = w.at[cl, sec, zb]
            arrive(rw.at[cl, zb], piece)
            if k <= 2:
                send(piece, piece, swb.at[cl, k], rw.at[cl, zb], dev(dz=-sgn))
            send(piece, piece, swd.at[cl, zb], rwd.at[cl, zb], (1 - sec, i, t))

    def near():
        kv_along_x(kv_here(-1))
        kv_along_x(kv_here(1))
        left = kv_here(-2)
        send(kv.at[x, left], kv.at[x, left], skz.at[4], rkz.at[left], dev(dz=1))
        right = kv_here(2)
        send(kv.at[x, right], kv.at[x, right], skz.at[5], rkz.at[right], dev(dz=-1))
        far = zmod(z - 2 * sgn)
        send(kv.at[x, far], kv.at[x, far], skz.at[6], rkz.at[far], dev(dz=2 * sgn))
        kv_along_x(left)
        kv_along_x(right)

    def distant():
        kv_along_x(kv_here(-3))
        kv_along_x(kv_here(3))
        kv_along_x(kv_here(4))

    def before():
        @pl.when(x >= 1)
        def _():
            def one(zz, c):
                arrive(rk1.at[zz], kv.at[x - 1, zz])
                return c

            lax.fori_loop(0, NZ, one, 0)

    def second(h):
        @pl.when(x >= 1)
        def _():
            unit(1, h)

    def rest_of(h):
        unit(0, h)

    own_out(0)
    for load in loads[3:5]:
        load.wait()
    row = i * ROWS + lax.broadcasted_iota(jnp.int32, (ROWS, 1), 0)
    starts, ends, at = [], [], jnp.int32(0)
    for d in range(4):
        starts.append(at)
        at = at + doc_ref[0, d] * BLK
        ends.append(at)
    member = [(row >= starts[d]) & (row < ends[d]) for d in range(4)]
    first = jnp.zeros((ROWS, 1), jnp.int32)
    for d in range(4):
        first = jnp.where(member[d], starts[d], first)
    limit = (row // BLK + 1) * BLK

    lane = lax.broadcasted_iota(jnp.int32, (ROWS, ROWS), 1)

    def home(zz):
        return jnp.where((zz <= z) | (x < 2), x, x - 2)

    bases = [home(zz) * NZ * ROWS + zz * ROWS for zz in range(NZ)]
    bases += [(x - 1) * NZ * ROWS + zz * ROWS for zz in range(NZ)]
    bases += [(x - 2) * NZ * ROWS + z * ROWS]
    for n, base in enumerate(bases):
        bias[:, n * ROWS : (n + 1) * ROWS] = jnp.where(
            (lane >= first - base) & (lane < limit - base), 0.0, NEG
        )

    for load in loads[5:]:
        load.wait()

    def unit(b, h):
        def cols(n):
            return pl.ds(pl.multiple_of((2 * h + n) * HEAD, HEAD), HEAD)

        q = jnp.concatenate([q_ref[:, cols(0)], q_ref[:, cols(1)]], axis=0)
        if b == 0:
            spots = [(home(zz), zz) for zz in range(NZ)]
            mask = bias[:, : NZ * ROWS]
        else:
            spots = [(x - 1, zz) for zz in range(NZ)] + [(jnp.maximum(x - 2, 0), z)]
            mask = bias[:, NZ * ROWS :]
        keys = jnp.concatenate([kv[xx, zz, 0] for xx, zz in spots], axis=0)
        vals = jnp.concatenate([kv[xx, zz, 1] for xx, zz in spots], axis=0)
        s = nt_dot(q, keys) * (HEAD ** -0.5 * LOG2E) + jnp.concatenate([mask, mask], axis=0)
        best = jnp.max(s, axis=1, keepdims=True)
        if b == 1:
            old = m_s[h][:, :1]
            best = jnp.maximum(best, old)
        p = jnp.exp2(s - best)
        total = jnp.sum(p, axis=1, keepdims=True)
        summed = jnp.dot(p.astype(jnp.bfloat16), vals, preferred_element_type=jnp.float32)
        if b == 1:
            alpha = jnp.exp2(old - best)
            total = total + alpha * l_s[h][:, :1]
            summed = summed + alpha * acc[h]
        m_s[h] = jnp.broadcast_to(best, (2 * ROWS, HEAD))
        l_s[h] = jnp.broadcast_to(total, (2 * ROWS, HEAD))
        acc[h] = summed

    def finish(h):
        second(h)
        done = (acc[h] / l_s[h]).astype(jnp.bfloat16)
        for n in range(2):
            ab[x, :, (2 * h + n) * HEAD : (2 * h + n + 1) * HEAD] = done[n * ROWS : (n + 1) * ROWS]
        piece = ab.at[x, :, pl.ds(2 * h * HEAD, 2 * HEAD)]
        for n, dx in enumerate((1, -1)):
            send(piece, piece, sa.at[h, n], ra.at[h, n], dev(dx=dx))

    def all_weights(cl):
        def one(zz, c):
            arrive(rwd.at[cl, zz], w.at[cl, 1 - sec, zz])
            return c

        lax.fori_loop(0, NZ, one, 0)

    def project(j):
        dx = (0, -1, 1, 0)[j]
        cl = j // 3
        xx = (x + dx + NX) % NX
        if dx:
            for h in range(4):
                arrive(ra.at[h, j - 1], ab.at[xx, :, pl.ds(2 * h * HEAD, 2 * HEAD)])
        for s2 in range(2):
            o = nt_dot(ab[xx], w[cl, s2].reshape(512, 1024))
            ob[j, s2] = o.astype(jnp.bfloat16)
            to = 2 * s2 + ((x + 2 * cl) % NX) // 2
            lo = x % 2
            if dx:
                send(ob.at[j, s2], rb.at[lo, t], so.at[j, s2], ro.at[lo, t], (sec, xx * NZ + z, to))
            else:
                @pl.when(to == t)
                def _():
                    pltpu.make_async_copy(ob.at[j, s2], rb.at[lo, t], ro.at[lo, t]).start()

                @pl.when(to != t)
                def _():
                    send(ob.at[j, s2], rb.at[lo, t], so.at[j, s2], ro.at[lo, t], (sec, i, to))

    near()
    old_first()
    ring(0,1)
    across()
    distant()
    old_second()
    ring(0,2)
    own_out(1)
    old_last()
    rest_of(0)
    rest_of(1)
    ring(0,3)
    rest_of(2)
    rest_of(3)
    ring(1,1)
    before()
    finish(0)
    finish(1)
    ring(0,4)
    finish(2)
    finish(3)
    ring(1,2)
    all_weights(0)
    project(0)
    ring(1,3)
    project(1)
    project(2)
    ring(1,4)
    all_weights(1)
    project(3)
    squares = jnp.zeros((ROWS, 128), jnp.float32)
    for lo in range(2):
        for ts in range(NT):
            arrive(ro.at[lo, ts], rb.at[lo, ts])
        for c in range(4):
            cols = slice(c * 128, c * 128 + 128)
            wide = slice(lo * 512 + c * 128, lo * 512 + c * 128 + 128)
            h = res_ref[:, wide].astype(jnp.float32)
            for ts in range(NT):
                h = h + rb[lo, ts, :, cols].astype(jnp.float32)
            hid[:, wide] = h
            squares = squares + h * h
    column = jnp.broadcast_to(jnp.sum(squares, axis=1, keepdims=True), (ROWS, 128))
    sq[t] = jnp.transpose(column)[:8]
    for n, d in enumerate((1, 2, 3)):
        send(sq.at[t], sq.at[t], ss.at[n], rs.at[n], (sec, i, (t + d) % NT))
    gains = []
    for d in range(4):
        gains.append(gain_ref[...] * (1.0 + shift_ref[pl.ds(noise_ref[0, d], 1), :]))
    for n in range(7):
        arrive(skz.at[n], kv.at[0, 0])

    def drain(zz, c):
        for cl in range(2):
            arrive(swd.at[cl, zz], w.at[0, 0, 0])

        @pl.when(x < NX - 1)
        def _():
            arrive(skx1.at[zz], kv.at[0, 0])

        return c

    lax.fori_loop(0, NZ, drain, 0)
    arrive(swx.at[0], w.at[0, 0, 0])
    for cl in range(2):
        for k in range(4):
            arrive(swf.at[cl, k], w.at[0, 0, 0])
        for k in range(3):
            arrive(swb.at[cl, k], w.at[0, 0, 0])
    for h in range(4):
        for n in range(2):
            arrive(sa.at[h, n], ab.at[0, :, pl.ds(0, 2 * HEAD)])
    for s2 in range(2):
        for cl in range(2):
            @pl.when(2 * s2 + ((x + 2 * cl) % NX) // 2 != t)
            def _():
                arrive(so.at[3 * cl, s2], rb.at[0, 0])

        for j in (1, 2):
            arrive(so.at[j, s2], rb.at[0, 0])

    @pl.when(x < NX - 2)
    def _():
        arrive(sxx.at[0], kv.at[0, 0])

    def sent(cond, n):
        @pl.when(cond)
        def _():
            arrive(sk2.at[n], kv.at[0, 0])

    sent(need(z, 1), 0)
    sent(need(z, -1), 1)
    sent(by_two(z, 1), 2)
    sent(by_two(z, -1), 3)
    sent(need(zmod(z - 2), 3), 4)
    sent(need(zmod(z + 2), -3), 5)
    sent(need(zmod(z - 2 * sgn), 4), 6)

    for n, d in enumerate((1, 2, 3)):
        arrive(rs.at[n], sq.at[(t - d + NT) % NT])
    for n in range(3):
        arrive(ss.at[n], sq.at[0])
    whole = sq[0] + sq[1] + sq[2] + sq[3]
    inverse = jnp.transpose(jnp.broadcast_to(lax.rsqrt(whole[:1] / D + 1e-6), (ROWS, 128)))
    stores = []
    for c in range(8):
        cols = slice(c * 128, c * 128 + 128)
        g = jnp.broadcast_to(gains[0][:, cols], (ROWS, 128))
        for d in range(1, 4):
            g = jnp.where(member[d], gains[d][:, cols], g)
        result[:, cols] = (hid[:, cols] * inverse * g).astype(jnp.bfloat16)
        if c % 4 == 3:
            block = slice(c * 128 - 384, c * 128 + 128)
            stores.append(pltpu.make_async_copy(result.at[:, block], out_ref.at[:, block], sout.at[c // 4]))
            stores[-1].start()
    for store in stores:
        store.wait()


def on_device(queries, keys, values, residual, out_weight, norm_gain, level_shift, doc_lengths, noise_level):
    bf, f32, sem = jnp.bfloat16, jnp.float32, pltpu.SemaphoreType.DMA
    vm = pl.BlockSpec(memory_space=pltpu.VMEM)
    hbm = pl.BlockSpec(memory_space=pltpu.MemorySpace.HBM)
    return pl.pallas_call(
        kernel,
        out_shape=jax.ShapeDtypeStruct((ROWS, 1024), bf),
        in_specs=[hbm] * 9,
        out_specs=hbm,
        scratch_shapes=[
            pltpu.SMEM((1, 4), jnp.int32),
            pltpu.SMEM((1, 4), jnp.int32),
            pltpu.VMEM((ROWS, 1024), bf),
            pltpu.VMEM((ROWS, 1024), bf),
            pltpu.VMEM((1, 1024), f32),
            pltpu.VMEM((8, 1024), f32),
            pltpu.VMEM((NX, NZ, 2, ROWS, HEAD), bf),
            pltpu.VMEM((2, 2, NZ, 64, 1024), bf),
            pltpu.VMEM((ROWS, 17 * ROWS), f32),
            pltpu.VMEM((4, 2 * ROWS, HEAD), f32),
            pltpu.VMEM((4, 2 * ROWS, HEAD), f32),
            pltpu.VMEM((4, 2 * ROWS, HEAD), f32),
            pltpu.VMEM((NX, ROWS, 1024), bf),
            pltpu.VMEM((4, 2, ROWS, 512), bf),
            pltpu.VMEM((2, NT, ROWS, 512), bf),
            pltpu.VMEM((ROWS, 1024), f32),
            pltpu.VMEM((NT, 8, 128), f32),
            sem((9,)), sem((7,)), sem((NZ,)), sem((1,)), sem((7,)),
            sem((1,)), sem((2, 4)), sem((2, 3)), sem((2, NZ)), sem((4, 2)), sem((4, 2)), sem((3,)),
            pltpu.VMEM((ROWS, 1024), bf), sem((2,)), sem((NZ,)), sem((NZ,)), sem((NZ,)),
            sem((1,)), sem((2, NZ)), sem((2, NZ)), sem((4, 2)), sem((2, NT)), sem((3,)),
        ],
        compiler_params=pltpu.CompilerParams(
            collective_id=0, has_side_effects=True, vmem_limit_bytes=64 << 20
        ),
    )(
        doc_lengths, noise_level, queries, keys, values, residual, out_weight.T,
        norm_gain.reshape(1, 1024), level_shift,
    )


def solution(mesh):
    placed = (
        P(("section", "srv"), "tp"),
        P(("section", "srv"), "tp"),
        P(("section", "srv"), "tp"),
        P(("section", "srv"), "tp"),
        P("tp", ("section", "srv")),
        P("tp"),
        P(None, "tp"),
        P("section", None),
        P("section", None),
    )
    return jax.shard_map(
        on_device,
        mesh=mesh,
        in_specs=placed,
        out_specs=P(("section", "srv"), "tp"),
        check_vma=False,
    )
```
